256 devices in a mesh: dp: 16 (over x, y), expert: 16 (over z, core).
Axes of the slice: x: 4, y: 4, z: 8, core: 2. Of those that a mesh axis runs over, the one named last changes fastest.
Arguments:
- tokens: bfloat16 [32768, 2048], P(('dp', 'expert')), may hold values from -70 to 70
- routing: int32 [32768, 2], P(('dp', 'expert')), may hold values from 0 to 15, all different within a row; in each aligned block of 128 rows (0 to 127, 128 to 255, ...) at most 20 rows name the same one
- probs: bfloat16 [32768, 2], P(('dp', 'expert')), may hold values from 0.099609375 to 1
- cotangent: bfloat16 [32768, 2048], P(('dp', 'expert')), may hold values from -70 to 70
- w_gate: bfloat16 [16, 2048, 512], P('expert'), may hold values from -0.125 to 0.125
- w_up: bfloat16 [16, 2048, 512], P('expert'), may hold values from -0.125 to 0.125
- w_down: bfloat16 [16, 512, 2048], P('expert'), may hold values from -0.25 to 0.25
Outputs:
- grad_gate: float32 [16, 2048, 512], P('expert', 'dp')
- grad_up: float32 [16, 2048, 512], P('expert', 'dp')
- grad_down: float32 [16, 512, 2048], P('expert', None, 'dp')
- input_grad: bfloat16 [32768, 2048], P(('dp', 'expert'))
- router_grad: bfloat16 [32768, 2], P(('dp', 'expert'))
The draws below stay inside these ranges and needn't reach their ends.
Inputs may be any that keep to these rules, and one draw needn't show every extreme that they name: `routing`: each row names 2 different experts. Among the 128 rows of one device no expert is named more than 20 times, a bound that some block reaches.
All inputs are finite; a program needn't handle non-finite values.
Results may differ from the reference program's by a relative error of at most 0.0065.
Values may be sent and summed in bfloat16 or wider, within the bound.
No kernel may reach another device: no remote copies, remote signals or barrier semaphores. Data moves between devices by JAX's collectives and lax.ppermute only.
A program may use at most 64 MiB of HBM per device.

```python
import math
import jax
import jax.numpy as jnp
import numpy as np
from jax import lax

D = 2048
FF = 512
TOK_DEV = 128
TOP = 2
EXPERTS = 16
CAP = 20
TOKENS = 32768
LEVELS = 4
N_DP = 16
N_EXPERT = 16


def shifted_rows(key, salt_value, row_count, col_count):
    first_key, second_key = jax.random.split(jax.random.fold_in(key, salt_value), 2)
    column = jnp.arange(col_count, dtype=jnp.float32) / (col_count - 1)
    spread = 10.0 ** column / 3.0
    shared = jnp.clip(jax.random.normal(first_key, (col_count,), jnp.float32), -3.0, 3.0)
    jitter = jnp.clip(jax.random.normal(second_key, (row_count, col_count), jnp.float32), -4.0, 4.0)
    values = 0.6 * shared[None, :] + jitter
    return (values * spread[None, :]).astype(jnp.bfloat16)


def draw_tokens(key, part):
    return shifted_rows(key, 11, TOKENS, D)


def draw_cotangent(key, part):
    return shifted_rows(key, 23, TOKENS, D)


def levels(own_key, extent, pieces, smallest, largest):
    factor_of = 1.0
    for dim, blocks in pieces:
        heights = jax.random.uniform(jax.random.fold_in(jax.random.fold_in(own_key, 6), dim), (blocks,), jnp.float32, smallest / len(pieces), largest / len(pieces))
        factor_of = factor_of * jnp.repeat(jnp.exp(heights), extent[dim] // blocks).reshape((-1,) + (1,) * (len(extent) - 1 - dim))
    return factor_of


def deal_out(key, own, number, rows, amount, top, bound, slope):
    ranking = jax.random.permutation(key, amount)
    packed, ordinary = load_shares(amount, rows * top, bound, slope, True), load_shares(amount, rows * top, bound, slope, False)
    places = jnp.arange(amount)

    def named(sizes, turn):
        used = int((sizes > 0).sum())
        fixed = max(1, used // 4)
        passed = fixed + (places - fixed + turn * (used - fixed)) % max(1, amount - fixed)
        return jnp.zeros((amount,), jnp.int32).at[ranking[jnp.where(places < fixed, places, passed)]].set(jnp.asarray(sizes, jnp.int32))

    sizes = jnp.where(number % 4 == 0, named(packed, number // 4), named(ordinary, number - number // 4 - 1))
    mixed = jax.random.permutation(jax.random.fold_in(own, 3), amount)
    source_of, sink = mixed[0:amount // 2 * 2:2], mixed[1:amount // 2 * 2:2]
    room = jnp.minimum(sizes[source_of] - 1, bound - sizes[sink]) // 2
    room = jnp.where((source_of == ranking[0]) | (sink == ranking[0]) | (sizes[sink] == 0), 0, jnp.maximum(room, 0))
    passed = jax.random.randint(jax.random.fold_in(own, 4), (amount // 2,), 0, 1 << 20) % (room + 1)
    sizes = sizes.at[source_of].add(-passed).at[sink].add(passed)
    labels = jnp.searchsorted(jnp.cumsum(sizes), jnp.arange(rows * top), side="right").astype(jnp.int32)
    listing = labels.reshape(top, rows).T
    listing = listing[jax.random.permutation(jax.random.fold_in(own, 1), rows)]
    turn = jax.random.randint(jax.random.fold_in(own, 2), (rows, 1), 0, top)
    return jnp.take_along_axis(listing, (jnp.arange(top)[None, :] + turn) % top, axis=1)


def load_shares(count, total, most, skew, full):
    portions = [(1 << 20) // math.isqrt(standing ** skew) + 1 for standing in range(1, count + 1)]
    largest = most if full else min(most, max(-(-total // count), total * portions[0] // sum(portions)))
    least = 1 if total - largest >= count - 1 else 0
    holding, spare = [largest] + [least] * (count - 1), total - largest - least * (count - 1)
    while spare > 0:
        free = [i for i in range(1, count) if holding[i] < largest] or [i for i in range(1, count) if holding[i] < most]
        pool, budget = sum([portions[i] for i in free]), spare
        for i in free:
            extra = min(most - holding[i], max(1, budget * portions[i] // pool), spare)
            holding[i] = holding[i] + extra
            spare = spare - extra
    return np.array(holding)


def normal_values(rng, dims, scale, reach, cuts=(), held_as=jnp.bfloat16):
    entries = jax.random.normal(rng, dims, jnp.float32) * scale
    if len(cuts) > 0:
        entries = levels(rng, dims, cuts, -0.22, 0.18) * entries
    return jnp.clip(entries, min=-reach, max=reach).astype(held_as)


def setup_inputs(seed: int = 0) -> dict:
    arg_keys = jax.random.split(jax.random.key(seed), 8)
    tokens = draw_tokens(jax.random.fold_in(arg_keys[7], 71), 0)
    routing_keys = jax.random.split(jax.random.fold_in(arg_keys[1], 1), TOKENS // TOK_DEV)
    routing_turns = jax.random.permutation(jax.random.fold_in(arg_keys[1], 3), TOKENS // TOK_DEV)
    routing = jax.vmap(lambda own, number: deal_out(jax.random.fold_in(arg_keys[1], 2), own, number, TOK_DEV, EXPERTS, TOP, CAP, 2))(routing_keys, routing_turns).reshape((TOKENS, TOP))
    probs = jnp.clip(0.099609375 + 0.9003906 * jax.random.uniform(arg_keys[2], (TOKENS, TOP), jnp.float32) ** levels(arg_keys[2], (TOKENS, TOP), ((0, 256),), -0.2, 0.2), 0.099609375, 1.0).astype(jnp.bfloat16)
    cotangent = draw_cotangent(jax.random.fold_in(arg_keys[7], 71), 0)
    w_gate = normal_values(arg_keys[4], (EXPERTS, D, FF), D ** -0.5, 0.125, ((0, 16),))
    w_up = normal_values(arg_keys[5], (EXPERTS, D, FF), D ** -0.5, 0.125, ((0, 16),))
    w_down = normal_values(arg_keys[6], (EXPERTS, FF, D), FF ** -0.5, 0.25, ((0, 16),))
    return {"tokens": tokens, "routing": routing, "probs": probs, "cotangent": cotangent, "w_gate": w_gate, "w_up": w_up, "w_down": w_down}


epsilon = 1e-6


def slot_index(routing_block):
    flattened = routing_block.reshape(-1)
    onehot = (flattened[:, None] == jnp.arange(EXPERTS, dtype=jnp.int32)[None, :]).astype(jnp.int32)
    before = jnp.cumsum(onehot, axis=0) - onehot
    return (flattened * CAP + jnp.sum(before * onehot, axis=1)).astype(jnp.int32)


def expert_pass(routed, cot_rows, prob_rows, gate_matrix, up_matrix, down_matrix):
    gate_pre = jnp.dot(routed, gate_matrix, preferred_element_type=jnp.float32)
    up_pre = jnp.dot(routed, up_matrix, preferred_element_type=jnp.float32)
    sigmoid = jax.nn.sigmoid(gate_pre)
    activated = gate_pre * sigmoid
    hidden = (activated * up_pre).astype(jnp.bfloat16)
    output = jnp.dot(hidden, down_matrix, preferred_element_type=jnp.float32)
    router_slots = jnp.sum(output * cot_rows.astype(jnp.float32), axis=1).astype(jnp.bfloat16)
    scaled = (prob_rows.astype(jnp.float32)[:, None] * cot_rows.astype(jnp.float32)).astype(jnp.bfloat16)
    hidden_grad = jnp.dot(scaled, down_matrix.T, preferred_element_type=jnp.float32)
    up_grad = (hidden_grad * activated).astype(jnp.bfloat16)
    gate_grad = (hidden_grad * up_pre * sigmoid * (1.0 + gate_pre * (1.0 - sigmoid))).astype(jnp.bfloat16)
    routed_grad = (jnp.dot(gate_grad, gate_matrix.T, preferred_element_type=jnp.float32)
                   + jnp.dot(up_grad, up_matrix.T, preferred_element_type=jnp.float32)).astype(jnp.bfloat16)
    scaling = 1.0 / (EXPERTS * CAP)
    grads = jnp.stack([jnp.dot(routed.T, gate_grad, preferred_element_type=jnp.float32),
                       jnp.dot(routed.T, up_grad, preferred_element_type=jnp.float32),
                       jnp.dot(scaled.T, hidden, preferred_element_type=jnp.float32)]) * scaling
    return routed_grad, router_slots, grads


def adasum(stacked):
    for halving in range(LEVELS):
        halfway = stacked.shape[0] // 2
        former = stacked[:halfway]
        latter = stacked[halfway:]
        inner_sum = jnp.sum(former * latter, axis=(2, 3))
        former_sq = jnp.sum(former * former, axis=(2, 3))
        latter_sq = jnp.sum(latter * latter, axis=(2, 3))
        former_coef = 1.0 - inner_sum / (2.0 * (former_sq + epsilon))
        latter_coef = 1.0 - inner_sum / (2.0 * (latter_sq + epsilon))
        stacked = former_coef[:, :, None, None] * former + latter_coef[:, :, None, None] * latter
    return stacked[0]


def take_rows(lookup, indices):
    return jnp.take(lookup, indices, axis=0, mode="fill", fill_value=0)


def reference(tokens, routing, probs, cotangent, w_gate, w_up, w_down):
    blocks = N_DP * N_EXPERT
    choices = TOK_DEV * TOP
    slot_total = EXPERTS * CAP
    destination = jax.vmap(slot_index)(routing.reshape(blocks, TOK_DEV, TOP))

    def invert(dest_row):
        return jnp.full((slot_total,), choices, jnp.int32).at[dest_row].set(jnp.arange(choices, dtype=jnp.int32))

    source = jax.vmap(invert)(destination)
    token_of = jnp.where(source < choices, source // TOP, TOK_DEV).astype(jnp.int32)
    tok_blocks = tokens.reshape(blocks, TOK_DEV, D)
    cot_blocks = cotangent.reshape(blocks, TOK_DEV, D)
    prob_blocks = probs.reshape(blocks, choices)

    def per_expert(expert):
        offset = (expert * CAP).astype(jnp.int32)
        tok_index = lax.dynamic_slice_in_dim(token_of, offset, CAP, 1)
        src_index = lax.dynamic_slice_in_dim(source, offset, CAP, 1)
        routed = jax.vmap(take_rows)(tok_blocks, tok_index).reshape(N_DP, N_EXPERT * CAP, D)
        cot_rows = jax.vmap(take_rows)(cot_blocks, tok_index).reshape(N_DP, N_EXPERT * CAP, D)
        prob_rows = jax.vmap(take_rows)(prob_blocks, src_index).reshape(N_DP, N_EXPERT * CAP)
        gate_matrix = w_gate[expert]
        up_matrix = w_up[expert]
        down_matrix = w_down[expert]

        def one_replica(inputs):
            return expert_pass(inputs[0], inputs[1], inputs[2], gate_matrix, up_matrix, down_matrix)

        routed_grad, router_slots, grads = lax.map(one_replica, (routed, cot_rows, prob_rows))
        return routed_grad, router_slots, adasum(grads)

    routed_grad, router_slots, combined = lax.map(per_expert, jnp.arange(EXPERTS, dtype=jnp.int32))
    block_ids = jnp.arange(blocks, dtype=jnp.int32)
    data_of = (block_ids // N_EXPERT)[:, None]
    peer_of = (block_ids % N_EXPERT)[:, None]
    expert_of = destination // CAP
    slot_of = destination % CAP
    arrived = routed_grad[expert_of, data_of, peer_of * CAP + slot_of]
    input_grad = jnp.sum(arrived.reshape(blocks, TOK_DEV, TOP, D).astype(jnp.float32), axis=2)
    input_grad = input_grad.astype(jnp.bfloat16).reshape(TOKENS, D)
    router_grad = router_slots[expert_of, data_of, peer_of * CAP + slot_of].reshape(TOKENS, TOP)
    grad_gate = combined[:, 0]
    grad_up = combined[:, 1]
    grad_down = jnp.transpose(combined[:, 2], (0, 2, 1))
    return grad_gate, grad_up, grad_down, input_grad, router_grad
```

```python
import functools

import jax
import jax.numpy as jnp
from jax import lax
from jax.experimental import pallas as pl
from jax.experimental.pallas import tpu as pltpu
from jax.sharding import PartitionSpec as P

epsilon = 1e-06
VMEM = pl.BlockSpec(memory_space=pltpu.VMEM)
F32 = jnp.float32
BF16 = jnp.bfloat16


def params(mib):
    return pltpu.CompilerParams(vmem_limit_bytes=mib << 20)


def iota(shape, dim):
    return lax.broadcasted_iota(jnp.int32, shape, dim)


def quotient(value, divisor, limit):
    factor = -(-(1 << 20) // divisor)
    assert all((v * factor) >> 20 == v // divisor for v in range(limit))
    return (value * factor) >> 20


def flag(condition):
    return jnp.where(condition, 1.0, 0.0)


def matmul(a, b, a_dim=1, b_dim=0, precision=None):
    return lax.dot_general(
        a, b, (((a_dim,), (b_dim,)), ((), ())), precision=precision, preferred_element_type=F32
    )


def occupants(routing_rows, expert_of, slot_of, tokens):
    first = flag(routing_rows[0:1, :] == expert_of)
    second = flag(routing_rows[1:2, :] == expert_of)
    named = first + second
    shape = (tokens, tokens)
    earlier = flag(iota(shape, 0) < iota(shape, 1)).astype(BF16)
    count = matmul(named.astype(BF16), earlier)
    taken = named * flag(count == slot_of.astype(F32))
    return taken, first, second


def dispatch_kernel(experts, capacity, routing_ref, probs_ref, tokens_ref, cot_ref, out_ref):
    tokens, width = tokens_ref.shape
    rows = out_ref.shape[0]
    row = iota((rows, tokens), 0)
    expert_of = quotient(row, 2 * capacity, rows)
    place = row - expert_of * (2 * capacity)
    is_cot = flag(place >= capacity)
    slot_of = jnp.where(place >= capacity, place - capacity, place)
    taken, first, second = occupants(routing_ref[...], expert_of, slot_of, tokens)
    probs = probs_ref[...].astype(F32)
    weight = first * probs[0:1, :] + second * probs[1:2, :]
    pick = jnp.concatenate(
        [(taken * (1.0 - is_cot)).astype(BF16), (taken * is_cot * weight).astype(BF16)], axis=1
    )
    step = 512
    for at in range(0, width, step):
        both = jnp.concatenate([tokens_ref[:, at : at + step], cot_ref[:, at : at + step]], axis=0)
        out_ref[:, at : at + step] = matmul(pick, both).astype(BF16)


def expert_kernel(
    experts, capacity, mixed_ref, gate_ref, up_ref, down_ref,
    blocks_ref, gate_grad_ref, up_grad_ref, router_ref, routed_ref, scaled_ref,
):
    slots, width = routed_ref.shape
    hidden_width = gate_ref.shape[1]
    rows = mixed_ref.shape[0]
    slot = iota((slots, rows), 0)
    source = slot + quotient(slot, capacity, slots) * capacity
    column = iota((slots, rows), 1)
    pick_routed = flag(column == source).astype(BF16)
    pick_scaled = flag(column == source + capacity).astype(BF16)
    step = 512
    for at in range(0, width, step):
        part = mixed_ref[:, at : at + step]
        routed_ref[:, at : at + step] = matmul(pick_routed, part).astype(BF16)
        scaled_ref[:, at : at + step] = matmul(pick_scaled, part).astype(BF16)
    routed = routed_ref[...]
    scaled = scaled_ref[...]
    gate_pre = matmul(routed, gate_ref[...])
    up_pre = matmul(routed, up_ref[...])
    hidden_grad = matmul(scaled, down_ref[...], 1, 1)
    sigmoid = 1.0 / (1.0 + jnp.exp(-gate_pre))
    activated = gate_pre * sigmoid
    hidden = (activated * up_pre).astype(BF16)
    up_grad = (hidden_grad * activated).astype(BF16)
    gate_grad = (hidden_grad * up_pre * sigmoid * (1.0 + gate_pre * (1.0 - sigmoid))).astype(BF16)
    gate_grad_ref[...] = gate_grad
    up_grad_ref[...] = up_grad
    dots = jnp.sum(hidden.astype(F32) * hidden_grad, axis=1, keepdims=True)
    router_ref[...] = jnp.broadcast_to(dots, router_ref.shape)
    shard = blocks_ref.shape[2]
    scaling = 1.0 / slots
    step = 4 * shard
    for m, (left, right_ref) in enumerate(
        ((gate_grad, routed_ref), (up_grad, routed_ref), (hidden, scaled_ref))
    ):
        left_t = left.T
        for at in range(0, width, step):
            grads = (matmul(left_t, right_ref[:, at : at + step]) * scaling).astype(BF16)
            for j in range(step // shard):
                blocks_ref[at // shard + j, m * hidden_width : (m + 1) * hidden_width, :] = grads[
                    :, j * shard : (j + 1) * shard
                ]


def return_kernel(experts, capacity, padded, gate_grad_ref, up_grad_ref, router_ref, gate_ref, up_ref, out_ref):
    slots = gate_grad_ref.shape[0]
    width = out_ref.shape[1]
    rows = out_ref.shape[0]
    lanes = router_ref.shape[1]
    row = iota((rows, slots), 0)
    block = quotient(row, padded, rows)
    place = row - block * padded
    slot = iota((rows, slots), 1)
    slot_block = quotient(slot, capacity, slots)
    spread = (flag(slot == block * capacity + place) * flag(place < capacity)).astype(BF16)
    same = flag(slot_block == block)
    high_rows = (same * flag(place == capacity)).astype(BF16)
    low_rows = (same * flag(place == capacity + 1)).astype(BF16)
    dots = router_ref[...]
    lane_slot = iota((slots, lanes), 0)
    own_lane = flag(
        iota((slots, lanes), 1) == lane_slot - quotient(lane_slot, capacity, slots) * capacity
    )
    high = dots.astype(BF16)
    low = (dots - high.astype(F32)).astype(BF16)
    own = own_lane.astype(BF16)
    extra = matmul(high_rows, high * own) + matmul(low_rows, low * own)
    gate_grad = gate_grad_ref[...]
    up_grad = up_grad_ref[...]
    step = 512
    for at in range(0, width, step):
        rows_grad = matmul(gate_grad, gate_ref[at : at + step, :], 1, 1) + matmul(
            up_grad, up_ref[at : at + step, :], 1, 1
        )
        spread_out = matmul(spread, rows_grad.astype(BF16))
        if at == 0:
            out_ref[:, lanes:step] = spread_out[:, lanes:].astype(BF16)
            out_ref[:, 0:lanes] = (spread_out[:, :lanes] + extra).astype(BF16)
        else:
            out_ref[:, at : at + step] = spread_out.astype(BF16)


def gather_back_kernel(experts, capacity, padded, routing_ref, probs_ref, arrived_ref, grad_ref, router_ref):
    tokens, width = grad_ref.shape
    rows = arrived_ref.shape[0]
    row = iota((rows, tokens), 0)
    expert_of = quotient(row, padded, rows)
    slot_of = row - expert_of * padded
    taken, first, second = occupants(routing_ref[...], expert_of, slot_of, tokens)
    taken = taken * flag(slot_of < capacity)
    pick = taken.T.astype(BF16)
    step = 512
    for at in range(0, width, step):
        grad_ref[:, at : at + step] = matmul(pick, arrived_ref[:, at : at + step]).astype(BF16)
    lanes = tokens
    square_row = iota((rows, rows), 0)
    square_col = iota((rows, rows), 1)
    block = quotient(square_row, padded, rows)
    from_block = quotient(square_col, padded, rows)
    from_place = square_col - from_block * padded
    fetch = flag(block == from_block) * (
        flag(from_place == capacity) + flag(from_place == capacity + 1)
    )
    spread = matmul(fetch.astype(BF16), arrived_ref[:, 0:lanes])
    lane = iota((rows, lanes), 1)
    dots = jnp.sum(spread * flag(lane == slot_of), axis=1, keepdims=True)
    probs = probs_ref[...].astype(F32)
    chosen = [
        jnp.sum(taken * which * dots, axis=0, keepdims=True) for which in (first, second)
    ]
    router_ref[...] = (jnp.concatenate(chosen, axis=0) / probs).astype(BF16)


def gram_kernel(replicas, arrived_ref, out_ref):
    kinds = 3
    hidden_width = arrived_ref.shape[1] // kinds
    lanes = arrived_ref.shape[2]
    group = 16
    rows = replicas * group
    square = (rows, rows)
    same = flag((iota(square, 0) & (group - 1)) == (iota(square, 1) & (group - 1)))
    member = flag((iota((rows, lanes), 0) >> 4) == iota((rows, lanes), 1))
    fold = flag((iota((replicas, rows), 1) >> 4) == iota((replicas, rows), 0))
    result = jnp.zeros((replicas, lanes), F32)
    for m in range(kinds):
        total = jnp.zeros(square, F32)
        for at in range(m * hidden_width, (m + 1) * hidden_width, 2 * group):
            left = arrived_ref[:, at : at + group, :].reshape(rows, lanes)
            right = arrived_ref[:, at + group : at + 2 * group, :].reshape(rows, lanes)
            both = jnp.concatenate([left, right], axis=1)
            total = total + matmul(both, both, 1, 1)
        folded = matmul(total * same, member, precision=lax.Precision.HIGHEST)
        gram = matmul(fold, folded, precision=lax.Precision.HIGHEST)
        result = result + (pltpu.roll(gram, m * replicas, 1) if m else gram)
    for j in range(out_ref.shape[0]):
        out_ref[j] = result


def combine_kernel(replicas, partial_ref, arrived_ref, gate_ref, up_ref, down_ref):
    kinds = 3
    lanes = partial_ref.shape[2]
    hidden_width = arrived_ref.shape[1] // kinds
    summed = partial_ref[0]
    for j in range(1, partial_ref.shape[0]):
        summed = summed + partial_ref[j]
    row = iota((replicas, lanes), 0)
    lane = iota((replicas, lanes), 1)
    diagonal = flag(row == lane)
    inside = flag(lane < replicas)
    for m in range(kinds):
        gram = (pltpu.roll(summed, lanes - m * replicas, 1) if m else summed) * inside
        weights = diagonal
        half = replicas // 2
        while half >= 1:
            across = pltpu.roll(gram, lanes - half, 1)
            below = pltpu.roll(gram, replicas - half, 0)
            corner = pltpu.roll(across, replicas - half, 0)
            coefs = []
            for axis in (0, 1):
                former_sq = jnp.sum(gram * diagonal, axis=axis, keepdims=True)
                latter_sq = jnp.sum(corner * diagonal, axis=axis, keepdims=True)
                inner_sum = jnp.sum(across * diagonal, axis=axis, keepdims=True)
                former_sq = jnp.maximum(former_sq, 0.0)
                latter_sq = jnp.maximum(latter_sq, 0.0)
                coefs.append(
                    (
                        1.0 - inner_sum / (2.0 * (former_sq + epsilon)),
                        1.0 - inner_sum / (2.0 * (latter_sq + epsilon)),
                    )
                )
            (former_row, latter_row), (former_col, latter_col) = coefs
            live = flag(row < half) * flag(lane < half)
            gram = live * (
                former_col * (gram * former_row + across * latter_row)
                + latter_col * (below * former_row + corner * latter_row)
            )
            weights = flag(row < half) * (
                former_col * weights + latter_col * pltpu.roll(weights, replicas - half, 0)
            )
            half //= 2
        scalars = [
            jnp.sum(weights * flag(lane == d), axis=(0, 1), keepdims=True) for d in range(replicas)
        ]
        step = 128
        for at in range(0, hidden_width, step):
            start = m * hidden_width + at
            total = scalars[0] * arrived_ref[0, start : start + step, :].astype(F32)
            for d in range(1, replicas):
                total = total + scalars[d] * arrived_ref[d, start : start + step, :].astype(F32)
            if m == 2:
                down_ref[at : at + step, :] = total
            else:
                (gate_ref, up_ref)[m][:, at : at + step] = total.T


def call(kernel, name, out_shapes, mib, scratch=()):
    return pl.pallas_call(
        kernel,
        name=name,
        out_shape=out_shapes,
        scratch_shapes=scratch,
        compiler_params=params(mib),
    )


def per_device(tokens, routing, probs, cotangent, w_gate, w_up, w_down):
    experts = lax.axis_size("expert")
    replicas = lax.axis_size("dp")
    rows_here, top_count = routing.shape
    width = tokens.shape[1]
    hidden_width = w_gate.shape[2]
    capacity = 5 * rows_here * top_count // (4 * experts)
    slots = experts * capacity
    padded = capacity + 4
    shard = width // replicas
    shape = jax.ShapeDtypeStruct
    routing_rows = routing.T
    prob_rows = probs.T
    gate, up, down = w_gate[0], w_up[0], w_down[0]

    send = call(
        functools.partial(dispatch_kernel, experts, capacity),
        "dispatch", shape((2 * slots, width), BF16), 32,
    )(routing_rows, prob_rows, tokens, cotangent)
    mixed = lax.all_to_all(
        send.reshape(experts, 2 * capacity, width), "expert", 0, 0, tiled=True
    ).reshape(2 * slots, width)
    blocks, gate_grad, up_grad, router = call(
        functools.partial(expert_kernel, experts, capacity),
        "expert",
        (
            shape((replicas, 3 * hidden_width, shard), BF16),
            shape((slots, hidden_width), BF16),
            shape((slots, hidden_width), BF16),
            shape((slots, 128), F32),
        ),
        56,
        (pltpu.VMEM((slots, width), BF16), pltpu.VMEM((slots, width), BF16)),
    )(mixed, gate, up, down)
    arrived = lax.all_to_all(blocks, "dp", 0, 0, tiled=True)
    back = call(
        functools.partial(return_kernel, experts, capacity, padded),
        "return_rows", shape((experts * padded, width), BF16), 40,
    )(gate_grad, up_grad, router, gate, up)
    came_back = lax.all_to_all(
        back.reshape(experts, padded, width), "expert", 0, 0, tiled=True
    ).reshape(experts * padded, width)
    input_grad, router_grad = call(
        functools.partial(gather_back_kernel, experts, capacity, padded),
        "gather_back",
        (shape((rows_here, width), BF16), shape((top_count, rows_here), BF16)),
        32,
    )(routing_rows, prob_rows, came_back)
    partial = call(
        functools.partial(gram_kernel, replicas),
        "gram", shape((replicas, replicas, 128), F32), 40,
    )(arrived)
    partials = lax.all_to_all(partial, "dp", 0, 0, tiled=True)
    grad_gate, grad_up, grad_down = call(
        functools.partial(combine_kernel, replicas),
        "combine",
        (
            shape((shard, hidden_width), F32),
            shape((shard, hidden_width), F32),
            shape((hidden_width, shard), F32),
        ),
        40,
    )(partials, arrived)
    return (grad_gate[None], grad_up[None], grad_down[None], input_grad, router_grad.T)


def solution(mesh):
    placed = (
        P(("dp", "expert"), None),
        P(("dp", "expert"), None),
        P(("dp", "expert"), None),
        P(("dp", "expert"), None),
        P("expert", None, None),
        P("expert", None, None),
        P("expert", None, None),
    )
    return jax.shard_map(
        per_device,
        mesh=mesh,
        in_specs=placed,
        out_specs=(
            P("expert", "dp", None),
            P("expert", "dp", None),
            P("expert", None, "dp"),
            P(("dp", "expert"), None),
            P(("dp", "expert"), None),
        ),
        check_vma=False,
    )
```

```python
import functools

import jax
import jax.numpy as jnp
from jax import lax
from jax.experimental import pallas as pl
from jax.experimental.pallas import tpu as pltpu
from jax.sharding import PartitionSpec as P

epsilon = 1e-06
VMEM = pl.BlockSpec(memory_space=pltpu.VMEM)
F32 = jnp.float32
BF16 = jnp.bfloat16


def params(mib):
    return pltpu.CompilerParams(vmem_limit_bytes=mib << 20)


def iota(shape, dim):
    return lax.broadcasted_iota(jnp.int32, shape, dim)


def quotient(value, divisor, limit):
    factor = -(-(1 << 20) // divisor)
    assert all((v * factor) >> 20 == v // divisor for v in range(limit))
    return (value * factor) >> 20


def flag(condition):
    return jnp.where(condition, 1.0, 0.0)


def matmul(a, b, a_dim=1, b_dim=0, precision=None):
    return lax.dot_general(
        a, b, (((a_dim,), (b_dim,)), ((), ())), precision=precision, preferred_element_type=F32
    )


def occupants(first_choice, second_choice, expert_of, slot_of, tokens):
    first = flag(first_choice == expert_of)
    second = flag(second_choice == expert_of)
    named = first + second
    shape = (tokens, tokens)
    earlier = flag(iota(shape, 0) < iota(shape, 1)).astype(BF16)
    count = matmul(named.astype(BF16), earlier)
    taken = named * flag(count == slot_of.astype(F32))
    return taken, first, second


def dispatch_kernel(
    capacity, routing_ref, probs_ref, tokens_ref, cot_ref, out_ref, both_ref, token_sem, cot_sem
):
    tokens, width = tokens_ref.shape
    token_copy = pltpu.make_async_copy(tokens_ref, both_ref.at[0:tokens, :], token_sem)
    cot_copy = pltpu.make_async_copy(cot_ref, both_ref.at[tokens : 2 * tokens, :], cot_sem)
    token_copy.start()
    cot_copy.start()
    rows = out_ref.shape[0]
    row = iota((rows, tokens), 0)
    expert_of = quotient(row, 2 * capacity, rows)
    place = row - expert_of * (2 * capacity)
    is_cot = flag(place >= capacity)
    slot_of = jnp.where(place >= capacity, place - capacity, place)
    routing = routing_ref[...]
    taken, first, second = occupants(routing[0:1, :], routing[1:2, :], expert_of, slot_of, tokens)
    probs = probs_ref[...].astype(F32)
    weight = first * probs[0:1, :] + second * probs[1:2, :]
    pick = jnp.concatenate(
        [(taken * (1.0 - is_cot)).astype(BF16), (taken * is_cot * weight).astype(BF16)], axis=1
    )
    token_copy.wait()
    cot_copy.wait()
    step = 512
    for at in range(0, width, step):
        out_ref[:, at : at + step] = matmul(pick, both_ref[:, at : at + step]).astype(BF16)
    out_ref[:, width:] = (taken * (1.0 - is_cot + is_cot * first)).astype(BF16)


def expert_kernel(
    blocks, capacity, mixed_ref, gate_ref, up_ref, down_ref,
    blocks_ref, back_ref, routed_ref, scaled_ref, rows_grad_ref, out_ref, made_ref, out_sem, made_sem,
):
    slots, width = routed_ref.shape
    hidden_width = gate_ref.shape[1]
    rows = mixed_ref.shape[0]
    step = 512
    for e in range(blocks):
        into = slice(e * capacity, (e + 1) * capacity)
        routed_ref[into, :] = mixed_ref[2 * e * capacity : (2 * e + 1) * capacity, 0:width]
        scaled_ref[into, :] = mixed_ref[(2 * e + 1) * capacity : (2 * e + 2) * capacity, 0:width]
    routed = routed_ref[...]
    scaled = scaled_ref[...]
    gate_pre = matmul(routed, gate_ref[...])
    up_pre = matmul(routed, up_ref[...])
    hidden_grad = matmul(scaled, down_ref[...], 1, 1)
    sigmoid = 1.0 / (1.0 + jnp.exp(-gate_pre))
    activated = gate_pre * sigmoid
    hidden = (activated * up_pre).astype(BF16)
    up_grad = (hidden_grad * activated).astype(BF16)
    gate_grad = (hidden_grad * up_pre * sigmoid * (1.0 + gate_pre * (1.0 - sigmoid))).astype(BF16)
    dots = jnp.sum(hidden.astype(F32) * hidden_grad, axis=1, keepdims=True)
    for at in range(0, width, step):
        rows_grad_ref[:, at : at + step] = (
            matmul(gate_grad, gate_ref[at : at + step, :], 1, 1)
            + matmul(up_grad, up_ref[at : at + step, :], 1, 1)
        ).astype(BF16)
    part = mixed_ref[:, width:]
    tokens = part.shape[1]
    slot = iota((slots, rows), 0)
    source = slot + quotient(slot, capacity, slots) * capacity
    column = iota((slots, rows), 1)
    taken = matmul(flag(column == source).astype(BF16), part)
    first = matmul(flag(column == source + capacity).astype(BF16), part)
    second = taken - first
    block_of = quotient(iota((slots, tokens), 0), capacity, slots)
    dot_rows = []
    for which in (first, second):
        value = which * dots
        high = value.astype(BF16).astype(F32)
        dot_rows.append((high, value - high))
    window = 32
    slots_out = out_ref.shape[0]
    copies = []
    for e in range(blocks):
        start = (capacity * e) // 16 * 16
        mine = flag(block_of[start : start + window, :] == e)
        place = (taken[start : start + window, :] * mine).T.astype(BF16)
        turn = e % slots_out
        if e >= slots_out:
            copies[e - slots_out].wait()
        for at in range(0, width, step):
            out_ref[turn, 0:tokens, at : at + step] = matmul(
                place, rows_grad_ref[start : start + window, at : at + step]
            ).astype(BF16)
        extra = [
            jnp.sum(dot_rows[which][part][start : start + window, :] * mine, axis=0, keepdims=True)
            for part in (0, 1)
            for which in (0, 1)
        ]
        extra = jnp.concatenate(extra + [jnp.zeros((4, tokens), F32)], axis=0)
        extra = jnp.concatenate([extra, jnp.zeros((8, width - tokens), F32)], axis=1)
        out_ref[turn, tokens : tokens + 8, :] = extra.astype(BF16)
        copy = pltpu.make_async_copy(out_ref.at[turn], back_ref.at[e], out_sem.at[turn])
        copy.start()
        copies.append(copy)
    shard = blocks_ref.shape[2]
    scaling = 1.0 / slots
    step = 4 * shard
    made = []
    for m, (left, right_ref) in enumerate(
        ((gate_grad, routed_ref), (up_grad, routed_ref), (hidden, scaled_ref))
    ):
        left_t = left.T
        for at in range(0, width, step):
            grads = (matmul(left_t, right_ref[:, at : at + step]) * scaling).astype(BF16)
            for j in range(step // shard):
                made_ref[at // shard + j, m * hidden_width : (m + 1) * hidden_width, :] = grads[
                    :, j * shard : (j + 1) * shard
                ]
            piece = (
                slice(at // shard, (at + step) // shard),
                slice(m * hidden_width, (m + 1) * hidden_width),
            )
            copy = pltpu.make_async_copy(
                made_ref.at[piece], blocks_ref.at[piece], made_sem.at[len(made)]
            )
            copy.start()
            made.append(copy)
    for copy in copies[-slots_out:] + made:
        copy.wait()


def gram_kernel(replicas, arrived_ref, out_ref):
    kinds = 3
    hidden_width = arrived_ref.shape[1] // kinds
    lanes = arrived_ref.shape[2]
    group = 16
    rows = replicas * group
    square = (rows, rows)
    same = flag((iota(square, 0) & (group - 1)) == (iota(square, 1) & (group - 1)))
    member = flag((iota((rows, lanes), 0) >> 4) == iota((rows, lanes), 1))
    fold = flag((iota((replicas, rows), 1) >> 4) == iota((replicas, rows), 0))
    result = jnp.zeros((replicas, lanes), F32)
    for m in range(kinds):
        pieces = [
            arrived_ref[:, at : at + group, :].reshape(rows, lanes)
            for at in range(m * hidden_width, (m + 1) * hidden_width, group)
        ]
        pieces = jnp.concatenate(pieces, axis=1)
        total = matmul(pieces, pieces, 1, 1)
        folded = matmul(total * same, member, precision=lax.Precision.HIGHEST)
        gram = matmul(fold, folded, precision=lax.Precision.HIGHEST)
        result = result + (pltpu.roll(gram, m * replicas, 1) if m else gram)
    for j in range(out_ref.shape[0]):
        out_ref[j] = result


def combine_kernel(
    replicas, partial_ref, arrived_hbm, back_hbm, probs_ref, gate_ref, up_ref, down_ref, grad_hbm, router_ref,
    arrived_ref, back_ref, arrived_sem, back_sem, grad_sem,
):
    tokens = grad_hbm.shape[0]
    third = arrived_hbm.shape[1] // 3
    loads = []
    for m in range(3):
        piece = (slice(None), slice(m * third, (m + 1) * third))
        loads.append(pltpu.make_async_copy(arrived_hbm.at[piece], arrived_ref.at[piece], arrived_sem.at[m]))
        loads[m].start()
    back_copy = pltpu.make_async_copy(back_hbm, back_ref, back_sem)
    back_copy.start()
    kinds = 3
    lanes = partial_ref.shape[2]
    hidden_width = arrived_ref.shape[1] // kinds
    summed = partial_ref[0]
    for j in range(1, partial_ref.shape[0]):
        summed = summed + partial_ref[j]
    row = iota((replicas, lanes), 0)
    lane = iota((replicas, lanes), 1)
    diagonal = flag(row == lane)
    inside = flag(lane < replicas)
    for m in range(kinds):
        gram = (pltpu.roll(summed, lanes - m * replicas, 1) if m else summed) * inside
        weights = diagonal
        half = replicas // 2
        while half >= 1:
            across = pltpu.roll(gram, lanes - half, 1)
            below = pltpu.roll(gram, replicas - half, 0)
            corner = pltpu.roll(across, replicas - half, 0)
            coefs = []
            for axis in (0, 1):
                former_sq = jnp.sum(gram * diagonal, axis=axis, keepdims=True)
                latter_sq = jnp.sum(corner * diagonal, axis=axis, keepdims=True)
                inner_sum = jnp.sum(across * diagonal, axis=axis, keepdims=True)
                former_sq = jnp.maximum(former_sq, 0.0)
                latter_sq = jnp.maximum(latter_sq, 0.0)
                coefs.append(
                    (
                        1.0 - inner_sum / (2.0 * (former_sq + epsilon)),
                        1.0 - inner_sum / (2.0 * (latter_sq + epsilon)),
                    )
                )
            (former_row, latter_row), (former_col, latter_col) = coefs
            live = flag(row < half) * flag(lane < half)
            gram = live * (
                former_col * (gram * former_row + across * latter_row)
                + latter_col * (below * former_row + corner * latter_row)
            )
            weights = flag(row < half) * (
                former_col * weights + latter_col * pltpu.roll(weights, replicas - half, 0)
            )
            half //= 2
        scalars = [
            jnp.sum(weights * flag(lane == d), axis=(0, 1), keepdims=True) for d in range(replicas)
        ]
        if m == 0:
            back_copy.wait()
            grad_copy = pltpu.make_async_copy(back_ref.at[0:tokens, :], grad_hbm, grad_sem)
            grad_copy.start()
        loads[m].wait()
        step = 128
        for at in range(0, hidden_width, step):
            start = m * hidden_width + at
            total = scalars[0] * arrived_ref[0, start : start + step, :].astype(F32)
            for d in range(1, replicas):
                total = total + scalars[d] * arrived_ref[d, start : start + step, :].astype(F32)
            if m == 2:
                down_ref[at : at + step, :] = total
            else:
                (gate_ref, up_ref)[m][:, at : at + step] = total.T
    dots = back_ref[tokens : tokens + 8, 0:tokens].astype(F32)
    router_ref[...] = ((dots[0:2, :] + dots[2:4, :]) / probs_ref[...].astype(F32)).astype(BF16)
    grad_copy.wait()


def call(kernel, name, out_shapes, mib, scratch=(), specs=None, out_specs=None):
    more = {}
    if specs is not None:
        more["in_specs"] = specs
    if out_specs is not None:
        more["out_specs"] = out_specs
    return pl.pallas_call(
        kernel,
        name=name,
        out_shape=out_shapes,
        scratch_shapes=scratch,
        compiler_params=params(mib),
        **more,
    )


def per_device(tokens, routing, probs, cotangent, w_gate, w_up, w_down):
    experts = lax.axis_size("expert")
    replicas = lax.axis_size("dp")
    rows_here, top_count = routing.shape
    width = tokens.shape[1]
    hidden_width = w_gate.shape[2]
    capacity = 5 * rows_here * top_count // (4 * experts)
    slots = experts * capacity
    shard = width // replicas
    shape = jax.ShapeDtypeStruct
    routing_rows = routing.T
    prob_rows = probs.T
    gate, up, down = w_gate[0], w_up[0], w_down[0]
    pinned = functools.partial(pltpu.with_memory_space_constraint, memory_space=pltpu.HBM)
    in_hbm = pl.BlockSpec(memory_space=pltpu.HBM)
    dma = pltpu.SemaphoreType.DMA

    send = call(
        functools.partial(dispatch_kernel, capacity),
        "dispatch", shape((2 * slots, width + rows_here), BF16), 16,
        (pltpu.VMEM((2 * rows_here, width), BF16), dma, dma),
        specs=[VMEM, VMEM, in_hbm, in_hbm],
    )(routing_rows, prob_rows, pinned(tokens), pinned(cotangent))
    mixed = lax.all_to_all(
        send.reshape(experts, 2 * capacity, width + rows_here), "expert", 0, 0, tiled=True
    ).reshape(2 * slots, width + rows_here)
    blocks, back = call(
        functools.partial(expert_kernel, experts, capacity),
        "expert",
        (
            pltpu.HBM((replicas, 3 * hidden_width, shard), BF16),
            pltpu.HBM((experts, rows_here + 8, width), BF16),
        ),
        36,
        (
            pltpu.VMEM((slots, width), BF16),
            pltpu.VMEM((slots, width), BF16),
            pltpu.VMEM((slots, width), BF16),
            pltpu.VMEM((4, rows_here + 8, width), BF16),
            pltpu.VMEM((replicas, 3 * hidden_width, shard), BF16),
            dma((4,)),
            dma((3 * width // 512,)),
        ),
        specs=[VMEM] * 4,
        out_specs=(in_hbm, in_hbm),
    )(mixed, gate, up, down)
    back = lax.psum_scatter(
        back.reshape(experts * (rows_here + 8), width), "expert", scatter_dimension=0, tiled=True
    )
    arrived = lax.all_to_all(blocks, "dp", 0, 0, tiled=True)
    partial = call(
        functools.partial(gram_kernel, replicas),
        "gram", shape((replicas, replicas, 128), F32), 20,
    )(arrived)
    partials = lax.all_to_all(partial, "dp", 0, 0, tiled=True)
    grad_gate, grad_up, grad_down, input_grad, router_grad = call(
        functools.partial(combine_kernel, replicas),
        "combine",
        (
            shape((shard, hidden_width), F32),
            shape((shard, hidden_width), F32),
            shape((hidden_width, shard), F32),
            pltpu.HBM((rows_here, width), BF16),
            shape((top_count, rows_here), BF16),
        ),
        16,
        (
            pltpu.VMEM((replicas, 3 * hidden_width, shard), BF16),
            pltpu.VMEM((rows_here + 8, width), BF16),
            dma((3,)),
            dma,
            dma,
        ),
        specs=[VMEM, in_hbm, in_hbm, VMEM],
        out_specs=(VMEM, VMEM, VMEM, in_hbm, VMEM),
    )(partials, pinned(arrived), pinned(back), prob_rows)
    return (grad_gate[None], grad_up[None], grad_down[None], input_grad, router_grad.T)


def solution(mesh):
    placed = (
        P(("dp", "expert"), None),
        P(("dp", "expert"), None),
        P(("dp", "expert"), None),
        P(("dp", "expert"), None),
        P("expert", None, None),
        P("expert", None, None),
        P("expert", None, None),
    )
    return jax.shard_map(
        per_device,
        mesh=mesh,
        in_specs=placed,
        out_specs=(
            P("expert", "dp", None),
            P("expert", "dp", None),
            P("expert", None, "dp"),
            P(("dp", "expert"), None),
            P(("dp", "expert"), None),
        ),
        check_vma=False,
    )
```

```python
import functools

import jax
import jax.numpy as jnp
from jax import lax
from jax.experimental import pallas as pl
from jax.experimental.pallas import tpu as pltpu
from jax.sharding import PartitionSpec as P

epsilon = 1e-06
VMEM = pl.BlockSpec(memory_space=pltpu.VMEM)
F32 = jnp.float32
BF16 = jnp.bfloat16
BACK_STEP = 512


def params(mib):
    return pltpu.CompilerParams(vmem_limit_bytes=mib << 20)


def iota(shape, dim):
    return lax.broadcasted_iota(jnp.int32, shape, dim)


def quotient(value, divisor, limit):
    factor = -(-(1 << 20) // divisor)
    assert all((v * factor) >> 20 == v // divisor for v in range(limit))
    return (value * factor) >> 20


def flag(condition):
    return jnp.where(condition, 1.0, 0.0)


def matmul(a, b, a_dim=1, b_dim=0, precision=None):
    return lax.dot_general(
        a, b, (((a_dim,), (b_dim,)), ((), ())), precision=precision, preferred_element_type=F32
    )


def occupants(first_choice, second_choice, expert_of, slot_of, tokens):
    first = flag(first_choice == expert_of)
    second = flag(second_choice == expert_of)
    named = first + second
    shape = (tokens, tokens)
    earlier = flag(iota(shape, 0) < iota(shape, 1)).astype(BF16)
    count = matmul(named.astype(BF16), earlier)
    taken = named * flag(count == slot_of.astype(F32))
    return taken, first, second


def dispatch_kernel(
    capacity, routing_hbm, probs_hbm, tokens_hbm, cot_hbm, out_ref,
    routing_ref, probs_ref, both_ref, small_sem, wide_sem,
):
    tokens, width = tokens_hbm.shape
    step = 512
    routing_copy = pltpu.make_async_copy(routing_hbm, routing_ref, small_sem.at[0])
    probs_copy = pltpu.make_async_copy(probs_hbm, probs_ref, small_sem.at[1])
    routing_copy.start()
    probs_copy.start()
    copies = []
    for at in range(0, width, step):
        pair = []
        for first_row, source in ((0, tokens_hbm), (tokens, cot_hbm)):
            pair.append(
                pltpu.make_async_copy(
                    source.at[:, at : at + step],
                    both_ref.at[first_row : first_row + tokens, at : at + step],
                    wide_sem.at[2 * len(copies) + len(pair)],
                )
            )
            pair[-1].start()
        copies.append(pair)
    experts = out_ref.shape[0]
    pair = 2 * capacity
    rows = experts * pair
    row = iota((rows, tokens), 0)
    expert_of = quotient(row, pair, rows)
    place = row - expert_of * pair
    is_cot = flag(place >= capacity)
    slot_of = jnp.where(place >= capacity, place - capacity, place)
    routing_copy.wait()
    probs_copy.wait()
    routing = routing_ref[...]
    taken, first, second = occupants(routing[0:1, :], routing[1:2, :], expert_of, slot_of, tokens)
    probs = probs_ref[...].astype(F32)
    weight = first * probs[0:1, :] + second * probs[1:2, :]
    pick = jnp.concatenate(
        [(taken * (1.0 - is_cot)).astype(BF16), (taken * is_cot * weight).astype(BF16)], axis=1
    )
    taken_bf = taken.astype(BF16)
    counted = (iota((1, tokens), 1) + 1).astype(F32)
    notes_at = width // tokens * pair
    out_ref[:, notes_at:, :] = jnp.zeros((experts, 8, tokens), BF16)
    for k in range(experts):
        heads = jnp.concatenate(
            [counted, flag(routing[0:1, :] == k), jnp.zeros((6, tokens), F32)], axis=0
        ).astype(BF16)
        notes = matmul(heads, taken_bf[pair * k : pair * (k + 1), :], 1, 1)
        out_ref[k, notes_at:, 0:pair] = notes.astype(BF16)
    for at, pair_of_copies in zip(range(0, width, step), copies):
        for copy in pair_of_copies:
            copy.wait()
        sent = matmul(pick, both_ref[:, at : at + step])
        for c in range(step // tokens):
            to = (at // tokens + c) * pair
            for k in range(experts):
                out_ref[k, to : to + pair, :] = sent[
                    pair * k : pair * (k + 1), c * tokens : (c + 1) * tokens
                ].astype(BF16)


def expert_kernel(
    capacity, mixed_ref, gate_ref, up_ref, down_ref,
    blocks_ref, back_ref, routed_ref, scaled_ref, rows_grad_ref, out_ref, made_ref, out_sem, made_sem,
):
    slots, width = routed_ref.shape
    hidden_width = gate_ref.shape[1]
    blocks = mixed_ref.shape[0]
    lanes = mixed_ref.shape[2]
    tokens = out_ref.shape[1] - 8
    pair = 2 * capacity
    for e in range(blocks):
        into = slice(e * capacity, (e + 1) * capacity)
        for c in range(width // lanes):
            columns = slice(c * lanes, (c + 1) * lanes)
            routed_ref[into, columns] = mixed_ref[e, c * pair : c * pair + capacity, :]
            scaled_ref[into, columns] = mixed_ref[e, c * pair + capacity : (c + 1) * pair, :]
    step = 512
    routed = routed_ref[...]
    scaled = scaled_ref[...]
    gate_pre = matmul(routed, gate_ref[...])
    up_pre = matmul(routed, up_ref[...])
    hidden_grad = matmul(scaled, down_ref[...], 1, 1)
    sigmoid = 1.0 / (1.0 + jnp.exp(-gate_pre))
    activated = gate_pre * sigmoid
    hidden = (activated * up_pre).astype(BF16)
    up_grad = (hidden_grad * activated).astype(BF16)
    gate_grad = (hidden_grad * up_pre * sigmoid * (1.0 + gate_pre * (1.0 - sigmoid))).astype(BF16)
    dots = jnp.sum(hidden.astype(F32) * hidden_grad, axis=1, keepdims=True)
    for at in range(0, width, step):
        rows_grad_ref[:, at : at + step] = (
            matmul(gate_grad, gate_ref[at : at + step, :], 1, 1)
            + matmul(up_grad, up_ref[at : at + step, :], 1, 1)
        ).astype(BF16)
    notes_at = width // lanes * pair
    notes = mixed_ref[:, notes_at : notes_at + 8, :].astype(F32).reshape(8 * blocks, lanes).astype(BF16)
    slot = iota((slots, lanes), 0)
    block_of = quotient(slot, capacity, slots)
    lane = iota((slots, lanes), 1)
    own_lane = flag(lane == slot - capacity * block_of)
    note_col = iota((slots, 8 * blocks), 1)
    note_block = quotient(iota((slots, 8 * blocks), 0), capacity, slots)
    named, leading = [
        jnp.sum(
            matmul(flag(note_col == 8 * note_block + j).astype(BF16), notes) * own_lane,
            axis=1, keepdims=True,
        )
        for j in (0, 1)
    ]
    taken = flag(iota((slots, tokens), 1).astype(F32) + 1.0 == named)
    first = taken * leading
    second = taken - first
    high = dots.astype(BF16).astype(F32)
    low = (dots - high).astype(BF16).astype(F32)
    extra_row = iota((8 * blocks, slots), 0)
    extra_same = flag((extra_row >> 3) == quotient(iota((8 * blocks, slots), 1), capacity, slots))
    extra = jnp.zeros((8 * blocks, tokens), F32)
    for j, (which, value) in enumerate(((first, high), (second, high), (first, low), (second, low))):
        extra = extra + matmul(
            (extra_same * flag((extra_row & 7) == j)).astype(BF16), (which * value).astype(BF16)
        )
    out_ref[:, tokens:, :] = jnp.zeros((blocks, 8, width), BF16)
    for e in range(blocks):
        out_ref[e, tokens:, 0:tokens] = extra[8 * e : 8 * e + 8, :].astype(BF16)
    taken_t = taken.T
    lane_block = quotient(iota((tokens, slots), 1), capacity, slots)
    split = min(blocks, 256 // capacity)
    windows = [(0, split, 0, min(slots, 256))]
    if split < blocks:
        windows.append((split, blocks, capacity * split // 128 * 128, slots))
    places = []
    for low_block, high_block, low_lane, high_lane in windows:
        lane_part = lane_block[:, low_lane:high_lane]
        place_part = taken_t[:, low_lane:high_lane]
        places.append(
            jnp.concatenate(
                [(place_part * flag(lane_part == e)).astype(BF16) for e in range(low_block, high_block)],
                axis=0,
            )
        )
    copies = []
    wide = BACK_STEP
    for at in range(0, width, wide):
        columns = slice(at, at + wide)
        for place, (low_block, high_block, low_lane, high_lane) in zip(places, windows):
            sent = matmul(place, rows_grad_ref[low_lane:high_lane, columns]).astype(BF16)
            out_ref[low_block:high_block, 0:tokens, columns] = sent.reshape(
                high_block - low_block, tokens, wide
            )
        copy = pltpu.make_async_copy(
            out_ref.at[:, :, columns], back_ref.at[:, :, columns], out_sem.at[len(copies)]
        )
        copy.start()
        copies.append(copy)
    shard = blocks_ref.shape[2]
    scaling = 1.0 / slots
    step = 4 * shard
    both_t = jnp.concatenate([gate_grad.T, up_grad.T], axis=0)
    made = []
    for left, right_ref, row in ((both_t, routed_ref, 0), (hidden.T, scaled_ref, 2 * hidden_width)):
        tall = left.shape[0]
        for at in range(0, width, step):
            grads = (matmul(left, right_ref[:, at : at + step]) * scaling).astype(BF16)
            for j in range(step // shard):
                made_ref[at // shard + j, row : row + tall, :] = grads[:, j * shard : (j + 1) * shard]
            piece = (slice(at // shard, (at + step) // shard), slice(row, row + tall))
            copy = pltpu.make_async_copy(
                made_ref.at[piece], blocks_ref.at[piece], made_sem.at[len(made)]
            )
            copy.start()
            made.append(copy)
    for copy in copies + made:
        copy.wait()


def gram_kernel(replicas, arrived_ref, out_ref):
    kinds = 3
    hidden_width = arrived_ref.shape[1] // kinds
    lanes = arrived_ref.shape[2]
    group = 16
    rows = replicas * group
    square = (rows, rows)
    same = flag((iota(square, 0) & (group - 1)) == (iota(square, 1) & (group - 1)))
    member = flag((iota((rows, lanes), 0) >> 4) == iota((rows, lanes), 1))
    fold = flag((iota((replicas, rows), 1) >> 4) == iota((replicas, rows), 0))
    result = jnp.zeros((replicas, lanes), F32)
    for m in range(kinds):
        pieces = [
            arrived_ref[:, at : at + group, :].reshape(rows, lanes)
            for at in range(m * hidden_width, (m + 1) * hidden_width, group)
        ]
        pieces = jnp.concatenate(pieces, axis=1)
        total = matmul(pieces, pieces, 1, 1)
        folded = matmul(total * same, member, precision=lax.Precision.HIGHEST)
        gram = matmul(fold, folded, precision=lax.Precision.HIGHEST)
        result = result + (pltpu.roll(gram, m * replicas, 1) if m else gram)
    for j in range(out_ref.shape[0]):
        out_ref[j] = result


def combine_kernel(
    replicas, partial_ref, arrived_hbm, back_hbm, probs_ref, gate_ref, up_ref, down_ref, grad_hbm, router_ref,
    arrived_ref, back_ref, arrived_sem, back_sem, grad_sem,
):
    tokens = grad_hbm.shape[0]
    third = arrived_hbm.shape[1] // 3
    loads = []
    for m in range(3):
        piece = (slice(None), slice(m * third, (m + 1) * third))
        loads.append(pltpu.make_async_copy(arrived_hbm.at[piece], arrived_ref.at[piece], arrived_sem.at[m]))
    for load in loads:
        load.start()
    back_copy = pltpu.make_async_copy(back_hbm, back_ref, back_sem)
    back_copy.start()
    kinds = 3
    lanes = partial_ref.shape[2]
    hidden_width = arrived_ref.shape[1] // kinds
    summed = partial_ref[0]
    for j in range(1, partial_ref.shape[0]):
        summed = summed + partial_ref[j]
    row = iota((replicas, lanes), 0)
    lane = iota((replicas, lanes), 1)
    diagonal = flag(row == lane)
    inside = flag(lane < replicas)
    for m in range(kinds):
        gram = (pltpu.roll(summed, lanes - m * replicas, 1) if m else summed) * inside
        weights = diagonal
        half = replicas // 2
        while half >= 1:
            across = pltpu.roll(gram, lanes - half, 1)
            below = pltpu.roll(gram, replicas - half, 0)
            corner = pltpu.roll(across, replicas - half, 0)
            coefs = []
            for axis in (0, 1):
                former_sq = jnp.sum(gram * diagonal, axis=axis, keepdims=True)
                latter_sq = jnp.sum(corner * diagonal, axis=axis, keepdims=True)
                inner_sum = jnp.sum(across * diagonal, axis=axis, keepdims=True)
                former_sq = jnp.maximum(former_sq, 0.0)
                latter_sq = jnp.maximum(latter_sq, 0.0)
                coefs.append(
                    (
                        1.0 - inner_sum / (2.0 * (former_sq + epsilon)),
                        1.0 - inner_sum / (2.0 * (latter_sq + epsilon)),
                    )
                )
            (former_row, latter_row), (former_col, latter_col) = coefs
            live = flag(row < half) * flag(lane < half)
            gram = live * (
                former_col * (gram * former_row + across * latter_row)
                + latter_col * (below * former_row + corner * latter_row)
            )
            weights = flag(row < half) * (
                former_col * weights + latter_col * pltpu.roll(weights, replicas - half, 0)
            )
            half //= 2
        scalars = [
            jnp.sum(weights * flag(lane == d), axis=(0, 1), keepdims=True) for d in range(replicas)
        ]
        loads[m].wait()
        if m == 2:
            back_copy.wait()
            grad_copy = pltpu.make_async_copy(back_ref.at[0:tokens, :], grad_hbm, grad_sem)
            grad_copy.start()
        step = 128
        for at in range(0, hidden_width, step):
            start = m * hidden_width + at
            total = scalars[0] * arrived_ref[0, start : start + step, :].astype(F32)
            for d in range(1, replicas):
                total = total + scalars[d] * arrived_ref[d, start : start + step, :].astype(F32)
            if m == 2:
                down_ref[at : at + step, :] = total
            else:
                (gate_ref, up_ref)[m][:, at : at + step] = total.T
    dots = back_ref[tokens : tokens + 8, 0:tokens].astype(F32)
    router_ref[...] = ((dots[0:2, :] + dots[2:4, :]) / probs_ref[...].astype(F32)).astype(BF16)
    grad_copy.wait()


def call(kernel, name, out_shapes, mib, scratch=(), specs=None, out_specs=None):
    more = {}
    if specs is not None:
        more["in_specs"] = specs
    if out_specs is not None:
        more["out_specs"] = out_specs
    return pl.pallas_call(
        kernel,
        name=name,
        out_shape=out_shapes,
        scratch_shapes=scratch,
        compiler_params=params(mib),
        **more,
    )


def per_device(tokens, routing, probs, cotangent, w_gate, w_up, w_down):
    experts = lax.axis_size("expert")
    replicas = lax.axis_size("dp")
    rows_here, top_count = routing.shape
    width = tokens.shape[1]
    hidden_width = w_gate.shape[2]
    capacity = 5 * rows_here * top_count // (4 * experts)
    slots = experts * capacity
    shard = width // replicas
    sent_rows = width // rows_here * 2 * capacity + 8
    shape = jax.ShapeDtypeStruct
    routing_rows = routing.T
    prob_rows = probs.T
    gate, up, down = w_gate[0], w_up[0], w_down[0]
    pinned = functools.partial(pltpu.with_memory_space_constraint, memory_space=pltpu.HBM)
    in_hbm = pl.BlockSpec(memory_space=pltpu.HBM)
    dma = pltpu.SemaphoreType.DMA

    send = call(
        functools.partial(dispatch_kernel, capacity),
        "dispatch", shape((experts, sent_rows, rows_here), BF16), 16,
        (
            pltpu.VMEM((top_count, rows_here), jnp.int32),
            pltpu.VMEM((top_count, rows_here), BF16),
            pltpu.VMEM((2 * rows_here, width), BF16),
            dma((2,)),
            dma((width // 256,)),
        ),
        specs=[in_hbm] * 4,
    )(pinned(routing_rows), pinned(prob_rows), pinned(tokens), pinned(cotangent))
    mixed = lax.all_to_all(send, "expert", 0, 0, tiled=True)
    blocks, back = call(
        functools.partial(expert_kernel, capacity),
        "expert",
        (
            pltpu.HBM((replicas, 3 * hidden_width, shard), BF16),
            pltpu.HBM((experts, rows_here + 8, width), BF16),
        ),
        44,
        (
            pltpu.VMEM((slots, width), BF16),
            pltpu.VMEM((slots, width), BF16),
            pltpu.VMEM((slots, width), BF16),
            pltpu.VMEM((experts, rows_here + 8, width), BF16),
            pltpu.VMEM((replicas, 3 * hidden_width, shard), BF16),
            dma((width // BACK_STEP,)),
            dma((2 * width // (4 * shard),)),
        ),
        specs=[VMEM] * 4,
        out_specs=(in_hbm, in_hbm),
    )(mixed, gate, up, down)
    back = lax.psum_scatter(
        back.reshape(experts * (rows_here + 8), width), "expert", scatter_dimension=0, tiled=True
    )
    arrived = lax.all_to_all(blocks, "dp", 0, 0, tiled=True)
    partial = call(
        functools.partial(gram_kernel, replicas),
        "gram", shape((replicas, replicas, 128), F32), 20,
    )(arrived)
    partials = lax.all_to_all(partial, "dp", 0, 0, tiled=True)
    grad_gate, grad_up, grad_down, input_grad, router_grad = call(
        functools.partial(combine_kernel, replicas),
        "combine",
        (
            shape((shard, hidden_width), F32),
            shape((shard, hidden_width), F32),
            shape((hidden_width, shard), F32),
            pltpu.HBM((rows_here, width), BF16),
            shape((top_count, rows_here), BF16),
        ),
        16,
        (
            pltpu.VMEM((replicas, 3 * hidden_width, shard), BF16),
            pltpu.VMEM((rows_here + 8, width), BF16),
            dma((3,)),
            dma,
            dma,
        ),
        specs=[VMEM, in_hbm, in_hbm, VMEM],
        out_specs=(VMEM, VMEM, VMEM, in_hbm, VMEM),
    )(partials, pinned(arrived), pinned(back), prob_rows)
    return (grad_gate[None], grad_up[None], grad_down[None], input_grad, router_grad.T)


def solution(mesh):
    placed = (
        P(("dp", "expert"), None),
        P(("dp", "expert"), None),
        P(("dp", "expert"), None),
        P(("dp", "expert"), None),
        P("expert", None, None),
        P("expert", None, None),
        P("expert", None, None),
    )
    return jax.shard_map(
        per_device,
        mesh=mesh,
        in_specs=placed,
        out_specs=(
            P("expert", "dp", None),
            P("expert", "dp", None),
            P("expert", None, "dp"),
            P(("dp", "expert"), None),
            P(("dp", "expert"), None),
        ),
        check_vma=False,
    )
```

```python
import functools

import jax
import jax.numpy as jnp
from jax import lax
from jax.experimental import pallas as pl
from jax.experimental.pallas import tpu as pltpu
from jax.sharding import PartitionSpec as P

epsilon = 1e-06
VMEM = pl.BlockSpec(memory_space=pltpu.VMEM)
F32 = jnp.float32
BF16 = jnp.bfloat16
BACK_STEP = 512


def params(mib):
    return pltpu.CompilerParams(vmem_limit_bytes=mib << 20)


def iota(shape, dim):
    return lax.broadcasted_iota(jnp.int32, shape, dim)


def quotient(value, divisor, limit):
    factor = -(-(1 << 20) // divisor)
    assert all((v * factor) >> 20 == v // divisor for v in range(limit))
    return (value * factor) >> 20


def flag(condition):
    return jnp.where(condition, 1.0, 0.0)


def matmul(a, b, a_dim=1, b_dim=0, precision=None):
    return lax.dot_general(
        a, b, (((a_dim,), (b_dim,)), ((), ())), precision=precision, preferred_element_type=F32
    )


def occupants(first_choice, second_choice, expert_of, slot_of, tokens):
    first = flag(first_choice == expert_of)
    second = flag(second_choice == expert_of)
    named = first + second
    shape = (tokens, tokens)
    earlier = flag(iota(shape, 0) < iota(shape, 1)).astype(BF16)
    count = matmul(named.astype(BF16), earlier)
    taken = named * flag(count == slot_of.astype(F32))
    return taken, first, second


def dispatch_kernel(
    capacity, routing_hbm, probs_hbm, tokens_hbm, cot_hbm, out_ref,
    routing_ref, probs_ref, both_ref, small_sem, wide_sem,
):
    tokens, width = tokens_hbm.shape
    step = 512
    routing_copy = pltpu.make_async_copy(routing_hbm, routing_ref, small_sem.at[0])
    probs_copy = pltpu.make_async_copy(probs_hbm, probs_ref, small_sem.at[1])
    routing_copy.start()
    probs_copy.start()
    copies = []
    for at in range(0, width, step):
        pair = []
        for first_row, source in ((0, tokens_hbm), (tokens, cot_hbm)):
            pair.append(
                pltpu.make_async_copy(
                    source.at[:, at : at + step],
                    both_ref.at[first_row : first_row + tokens, at : at + step],
                    wide_sem.at[2 * len(copies) + len(pair)],
                )
            )
            pair[-1].start()
        copies.append(pair)
    experts = out_ref.shape[0]
    pair = 2 * capacity
    rows = experts * pair
    row = iota((rows, tokens), 0)
    expert_of = quotient(row, pair, rows)
    place = row - expert_of * pair
    is_cot = flag(place >= capacity)
    slot_of = jnp.where(place >= capacity, place - capacity, place)
    routing_copy.wait()
    probs_copy.wait()
    routing = routing_ref[...]
    taken, first, second = occupants(routing[0:1, :], routing[1:2, :], expert_of, slot_of, tokens)
    probs = probs_ref[...].astype(F32)
    weight = first * probs[0:1, :] + second * probs[1:2, :]
    pick = jnp.concatenate(
        [(taken * (1.0 - is_cot)).astype(BF16), (taken * is_cot * weight).astype(BF16)], axis=1
    )
    taken_bf = taken.astype(BF16)
    counted = (iota((1, tokens), 1) + 1).astype(F32)
    notes_at = width // tokens * pair
    out_ref[:, notes_at:, :] = jnp.zeros((experts, 8, tokens), BF16)
    for k in range(experts):
        heads = jnp.concatenate(
            [counted, flag(routing[0:1, :] == k), jnp.zeros((6, tokens), F32)], axis=0
        ).astype(BF16)
        notes = matmul(heads, taken_bf[pair * k : pair * (k + 1), :], 1, 1)
        out_ref[k, notes_at:, 0:pair] = notes.astype(BF16)
    for at, pair_of_copies in zip(range(0, width, step), copies):
        for copy in pair_of_copies:
            copy.wait()
        sent = matmul(pick, both_ref[:, at : at + step])
        for c in range(step // tokens):
            to = (at // tokens + c) * pair
            for k in range(experts):
                out_ref[k, to : to + pair, :] = sent[
                    pair * k : pair * (k + 1), c * tokens : (c + 1) * tokens
                ].astype(BF16)


def expert_kernel(
    capacity, mixed_ref, gate_ref, up_ref, down_ref,
    blocks_ref, back_ref, routed_ref, scaled_ref, rows_grad_ref, out_ref, made_ref, out_sem, made_sem,
):
    slots, width = routed_ref.shape
    hidden_width = gate_ref.shape[1]
    blocks = mixed_ref.shape[0]
    lanes = mixed_ref.shape[2]
    tokens = out_ref.shape[1] - 8
    pair = 2 * capacity
    for e in range(blocks):
        into = slice(e * capacity, (e + 1) * capacity)
        for c in range(width // lanes):
            columns = slice(c * lanes, (c + 1) * lanes)
            routed_ref[into, columns] = mixed_ref[e, c * pair : c * pair + capacity, :]
            scaled_ref[into, columns] = mixed_ref[e, c * pair + capacity : (c + 1) * pair, :]
    step = 512
    routed = routed_ref[...]
    scaled = scaled_ref[...]
    gate_pre = matmul(routed, gate_ref[...])
    up_pre = matmul(routed, up_ref[...])
    hidden_grad = matmul(scaled, down_ref[...], 1, 1)
    sigmoid = 1.0 / (1.0 + jnp.exp(-gate_pre))
    activated = gate_pre * sigmoid
    hidden = (activated * up_pre).astype(BF16)
    up_grad = (hidden_grad * activated).astype(BF16)
    gate_grad = (hidden_grad * up_pre * sigmoid * (1.0 + gate_pre * (1.0 - sigmoid))).astype(BF16)
    dots = jnp.sum(hidden.astype(F32) * hidden_grad, axis=1, keepdims=True)
    for at in range(0, width, step):
        rows_grad_ref[:, at : at + step] = (
            matmul(gate_grad, gate_ref[at : at + step, :], 1, 1)
            + matmul(up_grad, up_ref[at : at + step, :], 1, 1)
        ).astype(BF16)
    notes_at = width // lanes * pair
    notes = mixed_ref[:, notes_at : notes_at + 8, :].astype(F32).reshape(8 * blocks, lanes).astype(BF16)
    slot = iota((slots, lanes), 0)
    block_of = quotient(slot, capacity, slots)
    lane = iota((slots, lanes), 1)
    own_lane = flag(lane == slot - capacity * block_of)
    note_col = iota((slots, 8 * blocks), 1)
    note_block = quotient(iota((slots, 8 * blocks), 0), capacity, slots)
    named, leading = [
        jnp.sum(
            matmul(flag(note_col == 8 * note_block + j).astype(BF16), notes) * own_lane,
            axis=1, keepdims=True,
        )
        for j in (0, 1)
    ]
    taken = flag(iota((slots, tokens), 1).astype(F32) + 1.0 == named)
    first = taken * leading
    second = taken - first
    high = dots.astype(BF16).astype(F32)
    low = (dots - high).astype(BF16).astype(F32)
    extra_row = iota((8 * blocks, slots), 0)
    extra_same = flag((extra_row >> 3) == quotient(iota((8 * blocks, slots), 1), capacity, slots))
    extra = jnp.zeros((8 * blocks, tokens), F32)
    for j, (which, value) in enumerate(((first, high), (second, high), (first, low), (second, low))):
        extra = extra + matmul(
            (extra_same * flag((extra_row & 7) == j)).astype(BF16), (which * value).astype(BF16)
        )
    out_ref[:, tokens:, :] = jnp.zeros((blocks, 8, width), BF16)
    for e in range(blocks):
        out_ref[e, tokens:, 0:tokens] = extra[8 * e : 8 * e + 8, :].astype(BF16)
    taken_t = taken.T
    lane_block = quotient(iota((tokens, slots), 1), capacity, slots)
    split = min(blocks, 256 // capacity)
    windows = [(0, split, 0, min(slots, 256))]
    if split < blocks:
        windows.append((split, blocks, capacity * split // 128 * 128, slots))
    places = []
    for low_block, high_block, low_lane, high_lane in windows:
        lane_part = lane_block[:, low_lane:high_lane]
        place_part = taken_t[:, low_lane:high_lane]
        places.append(
            jnp.concatenate(
                [(place_part * flag(lane_part == e)).astype(BF16) for e in range(low_block, high_block)],
                axis=0,
            )
        )
    copies = []
    wide = BACK_STEP
    for at in range(0, width, wide):
        columns = slice(at, at + wide)
        for place, (low_block, high_block, low_lane, high_lane) in zip(places, windows):
            sent = matmul(place, rows_grad_ref[low_lane:high_lane, columns]).astype(BF16)
            out_ref[low_block:high_block, 0:tokens, columns] = sent.reshape(
                high_block - low_block, tokens, wide
            )
        copy = pltpu.make_async_copy(
            out_ref.at[:, :, columns], back_ref.at[:, :, columns], out_sem.at[len(copies)]
        )
        copy.start()
        copies.append(copy)
    shard = blocks_ref.shape[2]
    scaling = 1.0 / slots
    step = 4 * shard
    both_t = jnp.concatenate([gate_grad.T, up_grad.T], axis=0)
    made = []
    for left, right_ref, row in ((both_t, routed_ref, 0), (hidden.T, scaled_ref, 2 * hidden_width)):
        tall = left.shape[0]
        for at in range(0, width, step):
            grads = (matmul(left, right_ref[:, at : at + step]) * scaling).astype(BF16)
            for j in range(step // shard):
                made_ref[at // shard + j, row : row + tall, :] = grads[:, j * shard : (j + 1) * shard]
            piece = (slice(at // shard, (at + step) // shard), slice(row, row + tall))
            copy = pltpu.make_async_copy(
                made_ref.at[piece], blocks_ref.at[piece], made_sem.at[len(made)]
            )
            copy.start()
            made.append(copy)
    for copy in copies + made:
        copy.wait()


def gram_kernel(replicas, arrived_ref, out_ref):
    kinds = 3
    hidden_width = arrived_ref.shape[1] // kinds
    lanes = arrived_ref.shape[2]
    group = 16
    rows = replicas * group
    square = (rows, rows)
    same = flag((iota(square, 0) & (group - 1)) == (iota(square, 1) & (group - 1)))
    member = flag((iota((rows, lanes), 0) >> 4) == iota((rows, lanes), 1))
    fold = flag((iota((replicas, rows), 1) >> 4) == iota((replicas, rows), 0))
    result = jnp.zeros((replicas, lanes), F32)
    totals = [jnp.zeros(square, F32) for _ in range(kinds)]
    size = hidden_width // 4
    for part in range(0, hidden_width, size):
        for m in range(kinds):
            base = m * hidden_width + part
            pieces = jnp.concatenate(
                [arrived_ref[:, at : at + group, :].reshape(rows, lanes) for at in range(base, base + size, group)],
                axis=1,
            )
            totals[m] = totals[m] + matmul(pieces, pieces, 1, 1)
    for m in range(kinds):
        total = totals[m]
        folded = matmul(total * same, member, precision=lax.Precision.HIGHEST)
        gram = matmul(fold, folded, precision=lax.Precision.HIGHEST)
        result = result + (pltpu.roll(gram, m * replicas, 1) if m else gram)
    for j in range(out_ref.shape[0]):
        out_ref[j] = result


def finish_kernel(back_hbm, probs_ref, grad_hbm, router_ref, back_ref, load_sem, store_sem):
    tokens, width = grad_hbm.shape
    parts = store_sem.shape[0]
    size = tokens // parts
    loads = [pltpu.make_async_copy(back_hbm.at[tokens:, :], back_ref.at[tokens:, :], load_sem.at[parts])]
    stores = []
    for part in range(parts):
        rows = slice(part * size, (part + 1) * size)
        loads.append(pltpu.make_async_copy(back_hbm.at[rows, :], back_ref.at[rows, :], load_sem.at[part]))
        stores.append(pltpu.make_async_copy(back_ref.at[rows, :], grad_hbm.at[rows, :], store_sem.at[part]))
    for load in loads:
        load.start()
    loads[0].wait()
    dots = back_ref[tokens:, 0:tokens].astype(F32)
    router_ref[...] = ((dots[0:2, :] + dots[2:4, :]) / probs_ref[...].astype(F32)).astype(BF16)
    for load, store in zip(loads[1:], stores):
        load.wait()
        store.start()
    for store in stores:
        store.wait()


def combine_kernel(replicas, partial_ref, arrived_ref, gate_ref, up_ref, down_ref):
    kinds = 3
    lanes = partial_ref.shape[2]
    hidden_width = arrived_ref.shape[1] // kinds
    summed = partial_ref[0]
    for j in range(1, partial_ref.shape[0]):
        summed = summed + partial_ref[j]
    row = iota((replicas, lanes), 0)
    lane = iota((replicas, lanes), 1)
    diagonal = flag(row == lane)
    inside = flag(lane < replicas)
    for m in range(kinds):
        gram = (pltpu.roll(summed, lanes - m * replicas, 1) if m else summed) * inside
        weights = diagonal
        half = replicas // 2
        while half >= 1:
            across = pltpu.roll(gram, lanes - half, 1)
            below = pltpu.roll(gram, replicas - half, 0)
            corner = pltpu.roll(across, replicas - half, 0)
            coefs = []
            for axis in (0, 1):
                former_sq = jnp.sum(gram * diagonal, axis=axis, keepdims=True)
                latter_sq = jnp.sum(corner * diagonal, axis=axis, keepdims=True)
                inner_sum = jnp.sum(across * diagonal, axis=axis, keepdims=True)
                former_sq = jnp.maximum(former_sq, 0.0)
                latter_sq = jnp.maximum(latter_sq, 0.0)
                coefs.append(
                    (
                        1.0 - inner_sum / (2.0 * (former_sq + epsilon)),
                        1.0 - inner_sum / (2.0 * (latter_sq + epsilon)),
                    )
                )
            (former_row, latter_row), (former_col, latter_col) = coefs
            live = flag(row < half) * flag(lane < half)
            gram = live * (
                former_col * (gram * former_row + across * latter_row)
                + latter_col * (below * former_row + corner * latter_row)
            )
            weights = flag(row < half) * (
                former_col * weights + latter_col * pltpu.roll(weights, replicas - half, 0)
            )
            half //= 2
        scalars = [
            jnp.sum(weights * flag(lane == d), axis=(0, 1), keepdims=True) for d in range(replicas)
        ]
        step = 128
        for at in range(0, hidden_width, step):
            start = m * hidden_width + at
            total = scalars[0] * arrived_ref[0, start : start + step, :].astype(F32)
            for d in range(1, replicas):
                total = total + scalars[d] * arrived_ref[d, start : start + step, :].astype(F32)
            if m == 2:
                down_ref[at : at + step, :] = total
            else:
                (gate_ref, up_ref)[m][:, at : at + step] = total.T


def call(kernel, name, out_shapes, mib, scratch=(), specs=None, out_specs=None):
    more = {}
    if specs is not None:
        more["in_specs"] = specs
    if out_specs is not None:
        more["out_specs"] = out_specs
    return pl.pallas_call(
        kernel,
        name=name,
        out_shape=out_shapes,
        scratch_shapes=scratch,
        compiler_params=params(mib),
        **more,
    )


def per_device(tokens, routing, probs, cotangent, w_gate, w_up, w_down):
    experts = lax.axis_size("expert")
    replicas = lax.axis_size("dp")
    rows_here, top_count = routing.shape
    width = tokens.shape[1]
    hidden_width = w_gate.shape[2]
    capacity = 5 * rows_here * top_count // (4 * experts)
    slots = experts * capacity
    shard = width // replicas
    sent_rows = width // rows_here * 2 * capacity + 8
    shape = jax.ShapeDtypeStruct
    routing_rows = routing.T
    prob_rows = probs.T
    gate, up, down = w_gate[0], w_up[0], w_down[0]
    pinned = functools.partial(pltpu.with_memory_space_constraint, memory_space=pltpu.HBM)
    in_hbm = pl.BlockSpec(memory_space=pltpu.HBM)
    dma = pltpu.SemaphoreType.DMA

    send = call(
        functools.partial(dispatch_kernel, capacity),
        "dispatch", shape((experts, sent_rows, rows_here), BF16), 16,
        (
            pltpu.VMEM((top_count, rows_here), jnp.int32),
            pltpu.VMEM((top_count, rows_here), BF16),
            pltpu.VMEM((2 * rows_here, width), BF16),
            dma((2,)),
            dma((width // 256,)),
        ),
        specs=[in_hbm] * 4,
    )(pinned(routing_rows), pinned(prob_rows), pinned(tokens), pinned(cotangent))
    mixed = lax.all_to_all(send, "expert", 0, 0, tiled=True)
    blocks, back = call(
        functools.partial(expert_kernel, capacity),
        "expert",
        (
            pltpu.HBM((replicas, 3 * hidden_width, shard), BF16),
            pltpu.HBM((experts, rows_here + 8, width), BF16),
        ),
        44,
        (
            pltpu.VMEM((slots, width), BF16),
            pltpu.VMEM((slots, width), BF16),
            pltpu.VMEM((slots, width), BF16),
            pltpu.VMEM((experts, rows_here + 8, width), BF16),
            pltpu.VMEM((replicas, 3 * hidden_width, shard), BF16),
            dma((width // BACK_STEP,)),
            dma((2 * width // (4 * shard),)),
        ),
        specs=[VMEM] * 4,
        out_specs=(in_hbm, in_hbm),
    )(mixed, gate, up, down)
    back = lax.psum_scatter(
        back.reshape(experts * (rows_here + 8), width), "expert", scatter_dimension=0, tiled=True
    )
    arrived = lax.all_to_all(blocks, "dp", 0, 0, tiled=True)
    partial = call(
        functools.partial(gram_kernel, replicas),
        "gram", shape((replicas, replicas, 128), F32), 12,
    )(arrived)
    partials = lax.all_to_all(partial, "dp", 0, 0, tiled=True)
    grad_gate, grad_up, grad_down = call(
        functools.partial(combine_kernel, replicas),
        "combine",
        (
            shape((shard, hidden_width), F32),
            shape((shard, hidden_width), F32),
            shape((hidden_width, shard), F32),
        ),
        12,
    )(partials, arrived)
    grad_gate, back = lax.optimization_barrier((grad_gate, back))
    input_grad, router_grad = call(
        finish_kernel,
        "finish",
        (pltpu.HBM((rows_here, width), BF16), shape((top_count, rows_here), BF16)),
        4,
        (pltpu.VMEM((rows_here + 8, width), BF16), dma((5,)), dma((4,))),
        specs=[in_hbm, VMEM],
        out_specs=(in_hbm, VMEM),
    )(pinned(back), prob_rows)
    return (grad_gate[None], grad_up[None], grad_down[None], input_grad, router_grad.T)


def solution(mesh):
    placed = (
        P(("dp", "expert"), None),
        P(("dp", "expert"), None),
        P(("dp", "expert"), None),
        P(("dp", "expert"), None),
        P("expert", None, None),
        P("expert", None, None),
        P("expert", None, None),
    )
    return jax.shard_map(
        per_device,
        mesh=mesh,
        in_specs=placed,
        out_specs=(
            P("expert", "dp", None),
            P("expert", "dp", None),
            P("expert", None, "dp"),
            P(("dp", "expert"), None),
            P(("dp", "expert"), None),
        ),
        check_vma=False,
    )
```

```python
import functools

import jax
import jax.numpy as jnp
from jax import lax
from jax.experimental import pallas as pl
from jax.experimental.pallas import tpu as pltpu
from jax.sharding import PartitionSpec as P

epsilon = 1e-06
VMEM = pl.BlockSpec(memory_space=pltpu.VMEM)
F32 = jnp.float32
BF16 = jnp.bfloat16
BACK_STEP = 512


def params(mib):
    return pltpu.CompilerParams(vmem_limit_bytes=mib << 20)


def iota(shape, dim):
    return lax.broadcasted_iota(jnp.int32, shape, dim)


def quotient(value, divisor, limit):
    factor = -(-(1 << 20) // divisor)
    assert all((v * factor) >> 20 == v // divisor for v in range(limit))
    return (value * factor) >> 20


def flag(condition):
    return jnp.where(condition, 1.0, 0.0)


def matmul(a, b, a_dim=1, b_dim=0, precision=None):
    return lax.dot_general(
        a, b, (((a_dim,), (b_dim,)), ((), ())), precision=precision, preferred_element_type=F32
    )


def occupants(first_choice, second_choice, expert_of, slot_of, tokens):
    first = flag(first_choice == expert_of)
    second = flag(second_choice == expert_of)
    named = first + second
    shape = (tokens, tokens)
    earlier = flag(iota(shape, 0) < iota(shape, 1)).astype(BF16)
    count = matmul(named.astype(BF16), earlier)
    taken = named * flag(count == slot_of.astype(F32))
    return taken, first, second


def dispatch_kernel(
    capacity, routing_hbm, probs_hbm, tokens_hbm, cot_hbm, out_ref,
    routing_ref, probs_ref, both_ref, small_sem, wide_sem,
):
    tokens, width = tokens_hbm.shape
    step = 1024
    routing_copy = pltpu.make_async_copy(routing_hbm, routing_ref, small_sem.at[0])
    probs_copy = pltpu.make_async_copy(probs_hbm, probs_ref, small_sem.at[1])
    routing_copy.start()
    probs_copy.start()
    copies = []
    for at in range(0, width, step):
        pair = []
        for first_row, source in ((0, tokens_hbm), (tokens, cot_hbm)):
            pair.append(
                pltpu.make_async_copy(
                    source.at[:, at : at + step],
                    both_ref.at[first_row : first_row + tokens, at : at + step],
                    wide_sem.at[2 * len(copies) + len(pair)],
                )
            )
            pair[-1].start()
        copies.append(pair)
    experts = out_ref.shape[0]
    pair = 2 * capacity
    rows = experts * pair
    row = iota((rows, tokens), 0)
    expert_of = quotient(row, pair, rows)
    place = row - expert_of * pair
    is_cot = flag(place >= capacity)
    slot_of = jnp.where(place >= capacity, place - capacity, place)
    routing_copy.wait()
    probs_copy.wait()
    routing = routing_ref[...]
    taken, first, second = occupants(routing[0:1, :], routing[1:2, :], expert_of, slot_of, tokens)
    probs = probs_ref[...].astype(F32)
    weight = first * probs[0:1, :] + second * probs[1:2, :]
    pick = jnp.concatenate(
        [(taken * (1.0 - is_cot)).astype(BF16), (taken * is_cot * weight).astype(BF16)], axis=1
    )
    taken_bf = taken.astype(BF16)
    counted = (iota((1, tokens), 1) + 1).astype(F32)
    notes_at = width // tokens * pair
    out_ref[:, notes_at:, :] = jnp.zeros((experts, 8, tokens), BF16)
    for k in range(experts):
        heads = jnp.concatenate(
            [counted, flag(routing[0:1, :] == k), jnp.zeros((6, tokens), F32)], axis=0
        ).astype(BF16)
        notes = matmul(heads, taken_bf[pair * k : pair * (k + 1), :], 1, 1)
        out_ref[k, notes_at:, 0:pair] = notes.astype(BF16)
    for at, pair_of_copies in zip(range(0, width, step), copies):
        for copy in pair_of_copies:
            copy.wait()
        sent = matmul(pick, both_ref[:, at : at + step])
        for c in range(step // tokens):
            to = (at // tokens + c) * pair
            for k in range(experts):
                out_ref[k, to : to + pair, :] = sent[
                    pair * k : pair * (k + 1), c * tokens : (c + 1) * tokens
                ].astype(BF16)


def expert_kernel(
    capacity, mixed_ref, gate_ref, up_ref, down_ref,
    blocks_ref, back_ref, routed_ref, scaled_ref, rows_grad_ref, out_ref, made_ref, out_sem, made_sem,
):
    slots, width = routed_ref.shape
    hidden_width = gate_ref.shape[1]
    blocks = mixed_ref.shape[0]
    lanes = mixed_ref.shape[2]
    tokens = out_ref.shape[1] - 8
    pair = 2 * capacity
    for e in range(blocks):
        into = slice(e * capacity, (e + 1) * capacity)
        for c in range(width // lanes):
            columns = slice(c * lanes, (c + 1) * lanes)
            routed_ref[into, columns] = mixed_ref[e, c * pair : c * pair + capacity, :]
            scaled_ref[into, columns] = mixed_ref[e, c * pair + capacity : (c + 1) * pair, :]
    step = 512
    routed = routed_ref[...]
    scaled = scaled_ref[...]
    gate_pre = matmul(routed, gate_ref[...])
    up_pre = matmul(routed, up_ref[...])
    hidden_grad = matmul(scaled, down_ref[...], 1, 1)
    sigmoid = 1.0 / (1.0 + jnp.exp(-gate_pre))
    activated = gate_pre * sigmoid
    hidden = (activated * up_pre).astype(BF16)
    up_grad = (hidden_grad * activated).astype(BF16)
    gate_grad = (hidden_grad * up_pre * sigmoid * (1.0 + gate_pre * (1.0 - sigmoid))).astype(BF16)
    dots = jnp.sum(hidden.astype(F32) * hidden_grad, axis=1, keepdims=True)
    for at in range(0, width, step):
        rows_grad_ref[:, at : at + step] = (
            matmul(gate_grad, gate_ref[at : at + step, :], 1, 1)
            + matmul(up_grad, up_ref[at : at + step, :], 1, 1)
        ).astype(BF16)
    notes_at = width // lanes * pair
    notes = mixed_ref[:, notes_at : notes_at + 8, :].astype(F32).reshape(8 * blocks, lanes).astype(BF16)
    slot = iota((slots, lanes), 0)
    block_of = quotient(slot, capacity, slots)
    lane = iota((slots, lanes), 1)
    own_lane = flag(lane == slot - capacity * block_of)
    note_col = iota((slots, 8 * blocks), 1)
    note_block = quotient(iota((slots, 8 * blocks), 0), capacity, slots)
    named, leading = [
        jnp.sum(
            matmul(flag(note_col == 8 * note_block + j).astype(BF16), notes) * own_lane,
            axis=1, keepdims=True,
        )
        for j in (0, 1)
    ]
    taken = flag(iota((slots, tokens), 1).astype(F32) + 1.0 == named)
    first = taken * leading
    second = taken - first
    high = dots.astype(BF16).astype(F32)
    low = (dots - high).astype(BF16).astype(F32)
    extra_row = iota((8 * blocks, slots), 0)
    extra_same = flag((extra_row >> 3) == quotient(iota((8 * blocks, slots), 1), capacity, slots))
    extra = jnp.zeros((8 * blocks, tokens), F32)
    for j, (which, value) in enumerate(((first, high), (second, high), (first, low), (second, low))):
        extra = extra + matmul(
            (extra_same * flag((extra_row & 7) == j)).astype(BF16), (which * value).astype(BF16)
        )
    out_ref[:, tokens:, :] = jnp.zeros((blocks, 8, width), BF16)
    for e in range(blocks):
        out_ref[e, tokens:, 0:tokens] = extra[8 * e : 8 * e + 8, :].astype(BF16)
    taken_t = taken.T
    lane_block = quotient(iota((tokens, slots), 1), capacity, slots)
    split = min(blocks, 256 // capacity)
    windows = [(0, split, 0, min(slots, 256))]
    if split < blocks:
        windows.append((split, blocks, capacity * split // 128 * 128, slots))
    places = []
    for low_block, high_block, low_lane, high_lane in windows:
        lane_part = lane_block[:, low_lane:high_lane]
        place_part = taken_t[:, low_lane:high_lane]
        places.append(
            jnp.concatenate(
                [(place_part * flag(lane_part == e)).astype(BF16) for e in range(low_block, high_block)],
                axis=0,
            )
        )
    copies = []
    wide = BACK_STEP
    for at in range(0, width, wide):
        columns = slice(at, at + wide)
        for place, (low_block, high_block, low_lane, high_lane) in zip(places, windows):
            sent = matmul(place, rows_grad_ref[low_lane:high_lane, columns]).astype(BF16)
            out_ref[low_block:high_block, 0:tokens, columns] = sent.reshape(
                high_block - low_block, tokens, wide
            )
        copy = pltpu.make_async_copy(
            out_ref.at[:, :, columns], back_ref.at[:, :, columns], out_sem.at[len(copies)]
        )
        copy.start()
        copies.append(copy)
    shard = blocks_ref.shape[2]
    scaling = 1.0 / slots
    step = 4 * shard
    both_t = jnp.concatenate([gate_grad.T, up_grad.T], axis=0)
    made = []
    for left, right_ref, row in ((both_t, routed_ref, 0), (hidden.T, scaled_ref, 2 * hidden_width)):
        tall = left.shape[0]
        for at in range(0, width, step):
            grads = (matmul(left, right_ref[:, at : at + step]) * scaling).astype(BF16)
            for j in range(step // shard):
                made_ref[at // shard + j, row : row + tall, :] = grads[:, j * shard : (j + 1) * shard]
            piece = (slice(at // shard, (at + step) // shard), slice(row, row + tall))
            copy = pltpu.make_async_copy(
                made_ref.at[piece], blocks_ref.at[piece], made_sem.at[len(made)]
            )
            copy.start()
            made.append(copy)
    for copy in copies + made:
        copy.wait()


def gram_kernel(replicas, arrived_ref, out_ref):
    kinds = 3
    hidden_width = arrived_ref.shape[1] // kinds
    lanes = arrived_ref.shape[2]
    group = 16
    rows = replicas * group
    square = (rows, rows)
    same = flag((iota(square, 0) & (group - 1)) == (iota(square, 1) & (group - 1)))
    member = flag((iota((rows, lanes), 0) >> 4) == iota((rows, lanes), 1))
    result = jnp.zeros((replicas, lanes), F32)
    totals = [jnp.zeros(square, F32) for _ in range(kinds)]
    size = hidden_width // 4
    for part in range(0, hidden_width, size):
        for m in range(kinds):
            base = m * hidden_width + part
            pieces = jnp.concatenate(
                [arrived_ref[:, at : at + group, :].reshape(rows, lanes) for at in range(base, base + size, group)],
                axis=1,
            )
            totals[m] = totals[m] + matmul(pieces, pieces, 1, 1)
    for m in range(kinds):
        total = totals[m]
        folded = jnp.sum((total * same).reshape(replicas, group, rows), axis=1)
        gram = matmul(folded, member, precision=lax.Precision.HIGHEST)
        result = result + (pltpu.roll(gram, m * replicas, 1) if m else gram)
    for j in range(out_ref.shape[0]):
        out_ref[j] = result


def finish_kernel(back_hbm, probs_ref, grad_hbm, router_ref, back_ref, load_sem, store_sem):
    tokens, width = grad_hbm.shape
    parts = store_sem.shape[0]
    size = tokens // parts
    loads = [pltpu.make_async_copy(back_hbm.at[tokens:, :], back_ref.at[tokens:, :], load_sem.at[parts])]
    stores = []
    for part in range(parts):
        rows = slice(part * size, (part + 1) * size)
        loads.append(pltpu.make_async_copy(back_hbm.at[rows, :], back_ref.at[rows, :], load_sem.at[part]))
        stores.append(pltpu.make_async_copy(back_ref.at[rows, :], grad_hbm.at[rows, :], store_sem.at[part]))
    for load in loads:
        load.start()
    loads[0].wait()
    dots = back_ref[tokens:, 0:tokens].astype(F32)
    router_ref[...] = ((dots[0:2, :] + dots[2:4, :]) / probs_ref[...].astype(F32)).astype(BF16)
    for load, store in zip(loads[1:], stores):
        load.wait()
        store.start()
    for store in stores:
        store.wait()


def combine_kernel(replicas, partial_ref, arrived_ref, gate_ref, up_ref, down_ref):
    kinds = 3
    lanes = partial_ref.shape[2]
    hidden_width = arrived_ref.shape[1] // kinds
    summed = partial_ref[0]
    for j in range(1, partial_ref.shape[0]):
        summed = summed + partial_ref[j]
    row = iota((replicas, lanes), 0)
    lane = iota((replicas, lanes), 1)
    diagonal = flag(row == lane)
    inside = flag(lane < replicas)
    for m in range(kinds):
        gram = (pltpu.roll(summed, lanes - m * replicas, 1) if m else summed) * inside
        weights = diagonal
        half = replicas // 2
        while half >= 1:
            across = pltpu.roll(gram, lanes - half, 1)
            below = pltpu.roll(gram, replicas - half, 0)
            corner = pltpu.roll(across, replicas - half, 0)
            coefs = []
            for axis in (0, 1):
                former_sq = jnp.sum(gram * diagonal, axis=axis, keepdims=True)
                latter_sq = jnp.sum(corner * diagonal, axis=axis, keepdims=True)
                inner_sum = jnp.sum(across * diagonal, axis=axis, keepdims=True)
                former_sq = jnp.maximum(former_sq, 0.0)
                latter_sq = jnp.maximum(latter_sq, 0.0)
                coefs.append(
                    (
                        1.0 - inner_sum / (2.0 * (former_sq + epsilon)),
                        1.0 - inner_sum / (2.0 * (latter_sq + epsilon)),
                    )
                )
            (former_row, latter_row), (former_col, latter_col) = coefs
            live = flag(row < half) * flag(lane < half)
            gram = live * (
                former_col * (gram * former_row + across * latter_row)
                + latter_col * (below * former_row + corner * latter_row)
            )
            weights = flag(row < half) * (
                former_col * weights + latter_col * pltpu.roll(weights, replicas - half, 0)
            )
            half //= 2
        scalars = [
            jnp.sum(weights * flag(lane == d), axis=(0, 1), keepdims=True) for d in range(replicas)
        ]
        step = 128
        for at in range(0, hidden_width, step):
            start = m * hidden_width + at
            total = scalars[0] * arrived_ref[0, start : start + step, :].astype(F32)
            for d in range(1, replicas):
                total = total + scalars[d] * arrived_ref[d, start : start + step, :].astype(F32)
            if m == 2:
                down_ref[at : at + step, :] = total
            else:
                (gate_ref, up_ref)[m][:, at : at + step] = total.T


def call(kernel, name, out_shapes, mib, scratch=(), specs=None, out_specs=None):
    more = {}
    if specs is not None:
        more["in_specs"] = specs
    if out_specs is not None:
        more["out_specs"] = out_specs
    return pl.pallas_call(
        kernel,
        name=name,
        out_shape=out_shapes,
        scratch_shapes=scratch,
        compiler_params=params(mib),
        **more,
    )


def per_device(tokens, routing, probs, cotangent, w_gate, w_up, w_down):
    experts = lax.axis_size("expert")
    replicas = lax.axis_size("dp")
    rows_here, top_count = routing.shape
    width = tokens.shape[1]
    hidden_width = w_gate.shape[2]
    capacity = 5 * rows_here * top_count // (4 * experts)
    slots = experts * capacity
    shard = width // replicas
    sent_rows = width // rows_here * 2 * capacity + 8
    shape = jax.ShapeDtypeStruct
    routing_rows = routing.T
    prob_rows = probs.T
    gate, up, down = w_gate[0], w_up[0], w_down[0]
    pinned = functools.partial(pltpu.with_memory_space_constraint, memory_space=pltpu.HBM)
    in_hbm = pl.BlockSpec(memory_space=pltpu.HBM)
    dma = pltpu.SemaphoreType.DMA

    send = call(
        functools.partial(dispatch_kernel, capacity),
        "dispatch", shape((experts, sent_rows, rows_here), BF16), 16,
        (
            pltpu.VMEM((top_count, rows_here), jnp.int32),
            pltpu.VMEM((top_count, rows_here), BF16),
            pltpu.VMEM((2 * rows_here, width), BF16),
            dma((2,)),
            dma((width // 256,)),
        ),
        specs=[in_hbm] * 4,
    )(pinned(routing_rows), pinned(prob_rows), pinned(tokens), pinned(cotangent))
    mixed = lax.all_to_all(send, "expert", 0, 0, tiled=True)
    blocks, back = call(
        functools.partial(expert_kernel, capacity),
        "expert",
        (
            pltpu.HBM((replicas, 3 * hidden_width, shard), BF16),
            pltpu.HBM((experts, rows_here + 8, width), BF16),
        ),
        44,
        (
            pltpu.VMEM((slots, width), BF16),
            pltpu.VMEM((slots, width), BF16),
            pltpu.VMEM((slots, width), BF16),
            pltpu.VMEM((experts, rows_here + 8, width), BF16),
            pltpu.VMEM((replicas, 3 * hidden_width, shard), BF16),
            dma((width // BACK_STEP,)),
            dma((2 * width // (4 * shard),)),
        ),
        specs=[VMEM] * 4,
        out_specs=(in_hbm, in_hbm),
    )(mixed, gate, up, down)
    back = lax.psum_scatter(
        back.reshape(experts * (rows_here + 8), width), "expert", scatter_dimension=0, tiled=True
    )
    arrived = lax.all_to_all(blocks, "dp", 0, 0, tiled=True)
    partial = call(
        functools.partial(gram_kernel, replicas),
        "gram", shape((replicas, replicas, 128), F32), 12,
    )(arrived)
    partials = lax.all_to_all(partial, "dp", 0, 0, tiled=True)
    grad_gate, grad_up, grad_down = call(
        functools.partial(combine_kernel, replicas),
        "combine",
        (
            shape((shard, hidden_width), F32),
            shape((shard, hidden_width), F32),
            shape((hidden_width, shard), F32),
        ),
        12,
    )(partials, arrived)
    grad_gate, back = lax.optimization_barrier((grad_gate, back))
    input_grad, router_grad = call(
        finish_kernel,
        "finish",
        (pltpu.HBM((rows_here, width), BF16), shape((top_count, rows_here), BF16)),
        4,
        (pltpu.VMEM((rows_here + 8, width), BF16), dma((5,)), dma((4,))),
        specs=[in_hbm, VMEM],
        out_specs=(in_hbm, VMEM),
    )(pinned(back), prob_rows)
    return (grad_gate[None], grad_up[None], grad_down[None], input_grad, router_grad.T)


def solution(mesh):
    placed = (
        P(("dp", "expert"), None),
        P(("dp", "expert"), None),
        P(("dp", "expert"), None),
        P(("dp", "expert"), None),
        P("expert", None, None),
        P("expert", None, None),
        P("expert", None, None),
    )
    return jax.shard_map(
        per_device,
        mesh=mesh,
        in_specs=placed,
        out_specs=(
            P("expert", "dp", None),
            P("expert", "dp", None),
            P("expert", None, "dp"),
            P(("dp", "expert"), None),
            P(("dp", "expert"), None),
        ),
        check_vma=False,
    )
```

```python
import functools

import jax
import jax.numpy as jnp
from jax import lax
from jax.experimental import pallas as pl
from jax.experimental.pallas import tpu as pltpu
from jax.sharding import PartitionSpec as P

epsilon = 1e-06
VMEM = pl.BlockSpec(memory_space=pltpu.VMEM)
F32 = jnp.float32
BF16 = jnp.bfloat16
BACK_STEP = 512


def params(mib):
    return pltpu.CompilerParams(vmem_limit_bytes=mib << 20)


def iota(shape, dim):
    return lax.broadcasted_iota(jnp.int32, shape, dim)


def quotient(value, divisor, limit):
    factor = -(-(1 << 20) // divisor)
    assert all((v * factor) >> 20 == v // divisor for v in range(limit))
    return (value * factor) >> 20


def flag(condition):
    return jnp.where(condition, 1.0, 0.0)


def matmul(a, b, a_dim=1, b_dim=0, precision=None):
    return lax.dot_general(
        a, b, (((a_dim,), (b_dim,)), ((), ())), precision=precision, preferred_element_type=F32
    )


def occupants(first_choice, second_choice, expert_of, slot_of, tokens):
    first = flag(first_choice == expert_of)
    second = flag(second_choice == expert_of)
    named = first + second
    shape = (tokens, tokens)
    earlier = flag(iota(shape, 0) < iota(shape, 1)).astype(BF16)
    count = matmul(named.astype(BF16), earlier)
    taken = named * flag(count == slot_of.astype(F32))
    return taken, first, second


def dispatch_kernel(
    capacity, routing_hbm, probs_hbm, tokens_hbm, cot_hbm, out_ref,
    routing_ref, probs_ref, both_ref, small_sem, wide_sem,
):
    tokens, width = tokens_hbm.shape
    step = 1024
    routing_copy = pltpu.make_async_copy(routing_hbm, routing_ref, small_sem.at[0])
    probs_copy = pltpu.make_async_copy(probs_hbm, probs_ref, small_sem.at[1])
    routing_copy.start()
    probs_copy.start()
    copies = []
    for at in range(0, width, step):
        pair = []
        for first_row, source in ((0, tokens_hbm), (tokens, cot_hbm)):
            pair.append(
                pltpu.make_async_copy(
                    source.at[:, at : at + step],
                    both_ref.at[first_row : first_row + tokens, at : at + step],
                    wide_sem.at[2 * len(copies) + len(pair)],
                )
            )
            pair[-1].start()
        copies.append(pair)
    experts = out_ref.shape[0]
    pair = 2 * capacity
    rows = experts * pair
    row = iota((rows, tokens), 0)
    expert_of = quotient(row, pair, rows)
    place = row - expert_of * pair
    is_cot = flag(place >= capacity)
    slot_of = jnp.where(place >= capacity, place - capacity, place)
    routing_copy.wait()
    probs_copy.wait()
    routing = routing_ref[...]
    taken, first, second = occupants(routing[0:1, :], routing[1:2, :], expert_of, slot_of, tokens)
    probs = probs_ref[...].astype(F32)
    weight = first * probs[0:1, :] + second * probs[1:2, :]
    pick = jnp.concatenate(
        [(taken * (1.0 - is_cot)).astype(BF16), (taken * is_cot * weight).astype(BF16)], axis=1
    )
    taken_bf = taken.astype(BF16)
    counted = (iota((1, tokens), 1) + 1).astype(F32)
    notes_at = width // tokens * pair
    out_ref[:, notes_at:, :] = jnp.zeros((experts, 8, tokens), BF16)
    for k in range(experts):
        heads = jnp.concatenate(
            [counted, flag(routing[0:1, :] == k), jnp.zeros((6, tokens), F32)], axis=0
        ).astype(BF16)
        notes = matmul(heads, taken_bf[pair * k : pair * (k + 1), :], 1, 1)
        out_ref[k, notes_at:, 0:pair] = notes.astype(BF16)
    for at, pair_of_copies in zip(range(0, width, step), copies):
        for copy in pair_of_copies:
            copy.wait()
        sent = matmul(pick, both_ref[:, at : at + step])
        for c in range(step // tokens):
            to = (at // tokens + c) * pair
            for k in range(experts):
                out_ref[k, to : to + pair, :] = sent[
                    pair * k : pair * (k + 1), c * tokens : (c + 1) * tokens
                ].astype(BF16)


def expert_kernel(
    capacity, mixed_ref, gate_ref, up_ref, down_ref,
    blocks_ref, back_ref, routed_ref, scaled_ref, rows_grad_ref, out_ref, made_ref, out_sem, made_sem,
):
    slots, width = routed_ref.shape
    hidden_width = gate_ref.shape[1]
    blocks = mixed_ref.shape[0]
    lanes = mixed_ref.shape[2]
    tokens = out_ref.shape[1] - 8
    pair = 2 * capacity
    for e in range(blocks):
        into = slice(e * capacity, (e + 1) * capacity)
        for c in range(width // lanes):
            columns = slice(c * lanes, (c + 1) * lanes)
            routed_ref[into, columns] = mixed_ref[e, c * pair : c * pair + capacity, :]
            scaled_ref[into, columns] = mixed_ref[e, c * pair + capacity : (c + 1) * pair, :]
    step = 512
    notes_at = width // lanes * pair
    notes = mixed_ref[:, notes_at : notes_at + 8, :].astype(F32).reshape(8 * blocks, lanes).astype(BF16)
    slot = iota((slots, lanes), 0)
    block_of = quotient(slot, capacity, slots)
    lane = iota((slots, lanes), 1)
    own_lane = flag(lane == slot - capacity * block_of)
    note_col = iota((slots, 8 * blocks), 1)
    note_block = quotient(iota((slots, 8 * blocks), 0), capacity, slots)
    named, leading = [
        jnp.sum(
            matmul(flag(note_col == 8 * note_block + j).astype(BF16), notes) * own_lane,
            axis=1, keepdims=True,
        )
        for j in (0, 1)
    ]
    taken = flag(iota((slots, tokens), 1).astype(F32) + 1.0 == named)
    first = taken * leading
    second = taken - first
    routed = routed_ref[...]
    scaled = scaled_ref[...]
    gate_pre = matmul(routed, gate_ref[...])
    up_pre = matmul(routed, up_ref[...])
    hidden_grad = matmul(scaled, down_ref[...], 1, 1)
    sigmoid = 1.0 / (1.0 + jnp.exp(-gate_pre))
    activated = gate_pre * sigmoid
    hidden = (activated * up_pre).astype(BF16)
    up_grad = (hidden_grad * activated).astype(BF16)
    gate_grad = (hidden_grad * up_pre * sigmoid * (1.0 + gate_pre * (1.0 - sigmoid))).astype(BF16)
    dots = jnp.sum(hidden.astype(F32) * hidden_grad, axis=1, keepdims=True)
    for at in range(0, width, step):
        rows_grad_ref[:, at : at + step] = (
            matmul(gate_grad, gate_ref[at : at + step, :], 1, 1)
            + matmul(up_grad, up_ref[at : at + step, :], 1, 1)
        ).astype(BF16)
    high = dots.astype(BF16).astype(F32)
    low = (dots - high).astype(BF16).astype(F32)
    extra_row = iota((8 * blocks, slots), 0)
    extra_same = flag((extra_row >> 3) == quotient(iota((8 * blocks, slots), 1), capacity, slots))
    extra = jnp.zeros((8 * blocks, tokens), F32)
    for j, (which, value) in enumerate(((first, high), (second, high), (first, low), (second, low))):
        extra = extra + matmul(
            (extra_same * flag((extra_row & 7) == j)).astype(BF16), (which * value).astype(BF16)
        )
    out_ref[:, tokens:, :] = jnp.zeros((blocks, 8, width), BF16)
    for e in range(blocks):
        out_ref[e, tokens:, 0:tokens] = extra[8 * e : 8 * e + 8, :].astype(BF16)
    taken_t = taken.T
    lane_block = quotient(iota((tokens, slots), 1), capacity, slots)
    split = min(blocks, 256 // capacity)
    windows = [(0, split, 0, min(slots, 256))]
    if split < blocks:
        windows.append((split, blocks, capacity * split // 128 * 128, slots))
    places = []
    for low_block, high_block, low_lane, high_lane in windows:
        lane_part = lane_block[:, low_lane:high_lane]
        place_part = taken_t[:, low_lane:high_lane]
        places.append(
            jnp.concatenate(
                [(place_part * flag(lane_part == e)).astype(BF16) for e in range(low_block, high_block)],
                axis=0,
            )
        )
    copies = []
    wide = BACK_STEP
    for at in range(0, width, wide):
        columns = slice(at, at + wide)
        for place, (low_block, high_block, low_lane, high_lane) in zip(places, windows):
            sent = matmul(place, rows_grad_ref[low_lane:high_lane, columns]).astype(BF16)
            out_ref[low_block:high_block, 0:tokens, columns] = sent.reshape(
                high_block - low_block, tokens, wide
            )
        copy = pltpu.make_async_copy(
            out_ref.at[:, :, columns], back_ref.at[:, :, columns], out_sem.at[len(copies)]
        )
        copy.start()
        copies.append(copy)
    shard = blocks_ref.shape[2]
    scaling = 1.0 / slots
    step = 8 * shard
    both_t = jnp.concatenate([gate_grad.T, up_grad.T], axis=0)
    made = []
    for left, right_ref, row in ((both_t, routed_ref, 0), (hidden.T, scaled_ref, 2 * hidden_width)):
        tall = left.shape[0]
        for at in range(0, width, step):
            grads = (matmul(left, right_ref[:, at : at + step]) * scaling).astype(BF16)
            for j in range(step // shard):
                made_ref[at // shard + j, row : row + tall, :] = grads[:, j * shard : (j + 1) * shard]
            piece = (slice(at // shard, (at + step) // shard), slice(row, row + tall))
            copy = pltpu.make_async_copy(
                made_ref.at[piece], blocks_ref.at[piece], made_sem.at[len(made)]
            )
            copy.start()
            made.append(copy)
    for copy in copies + made:
        copy.wait()


def gram_kernel(replicas, arrived_ref, out_ref):
    kinds = 3
    hidden_width = arrived_ref.shape[1] // kinds
    lanes = arrived_ref.shape[2]
    group = 16
    rows = replicas * group
    square = (rows, rows)
    same = flag((iota(square, 0) & (group - 1)) == (iota(square, 1) & (group - 1)))
    member = flag((iota((rows, lanes), 0) >> 4) == iota((rows, lanes), 1))
    result = jnp.zeros((replicas, lanes), F32)
    totals = [jnp.zeros(square, F32) for _ in range(kinds)]
    size = hidden_width // 4
    for part in range(0, hidden_width, size):
        for m in range(kinds):
            base = m * hidden_width + part
            pieces = jnp.concatenate(
                [arrived_ref[:, at : at + group, :].reshape(rows, lanes) for at in range(base, base + size, group)],
                axis=1,
            )
            totals[m] = totals[m] + matmul(pieces, pieces, 1, 1)
    for m in range(kinds):
        total = totals[m]
        folded = jnp.sum((total * same).reshape(replicas, group, rows), axis=1)
        gram = matmul(folded, member, precision=lax.Precision.HIGHEST)
        result = result + (pltpu.roll(gram, m * replicas, 1) if m else gram)
    for j in range(out_ref.shape[0]):
        out_ref[j] = result


def finish_kernel(back_hbm, probs_ref, grad_hbm, router_ref, back_ref, load_sem, store_sem):
    tokens, width = grad_hbm.shape
    parts = store_sem.shape[0]
    size = tokens // parts
    loads = [pltpu.make_async_copy(back_hbm.at[tokens:, :], back_ref.at[tokens:, :], load_sem.at[parts])]
    stores = []
    for part in range(parts):
        rows = slice(part * size, (part + 1) * size)
        loads.append(pltpu.make_async_copy(back_hbm.at[rows, :], back_ref.at[rows, :], load_sem.at[part]))
        stores.append(pltpu.make_async_copy(back_ref.at[rows, :], grad_hbm.at[rows, :], store_sem.at[part]))
    for load in loads:
        load.start()
    loads[0].wait()
    dots = back_ref[tokens:, 0:tokens].astype(F32)
    router_ref[...] = ((dots[0:2, :] + dots[2:4, :]) / probs_ref[...].astype(F32)).astype(BF16)
    for load, store in zip(loads[1:], stores):
        load.wait()
        store.start()
    for store in stores:
        store.wait()


def combine_kernel(replicas, partial_ref, arrived_ref, gate_ref, up_ref, down_ref):
    kinds = 3
    lanes = partial_ref.shape[2]
    hidden_width = arrived_ref.shape[1] // kinds
    summed = partial_ref[0]
    for j in range(1, partial_ref.shape[0]):
        summed = summed + partial_ref[j]
    row = iota((replicas, lanes), 0)
    lane = iota((replicas, lanes), 1)
    diagonal = flag(row == lane)
    inside = flag(lane < replicas)
    all_scalars = []
    for m in range(kinds):
        gram = (pltpu.roll(summed, lanes - m * replicas, 1) if m else summed) * inside
        weights = diagonal
        half = replicas // 2
        while half >= 1:
            across = pltpu.roll(gram, lanes - half, 1)
            below = pltpu.roll(gram, replicas - half, 0)
            corner = pltpu.roll(across, replicas - half, 0)
            coefs = []
            for axis in (0, 1):
                former_sq = jnp.sum(gram * diagonal, axis=axis, keepdims=True)
                latter_sq = jnp.sum(corner * diagonal, axis=axis, keepdims=True)
                inner_sum = jnp.sum(across * diagonal, axis=axis, keepdims=True)
                former_sq = jnp.maximum(former_sq, 0.0)
                latter_sq = jnp.maximum(latter_sq, 0.0)
                coefs.append(
                    (
                        1.0 - inner_sum / (2.0 * (former_sq + epsilon)),
                        1.0 - inner_sum / (2.0 * (latter_sq + epsilon)),
                    )
                )
            (former_row, latter_row), (former_col, latter_col) = coefs
            live = flag(row < half) * flag(lane < half)
            gram = live * (
                former_col * (gram * former_row + across * latter_row)
                + latter_col * (below * former_row + corner * latter_row)
            )
            weights = flag(row < half) * (
                former_col * weights + latter_col * pltpu.roll(weights, replicas - half, 0)
            )
            half //= 2
        all_scalars.append(
            [jnp.sum(weights * flag(lane == d), axis=(0, 1), keepdims=True) for d in range(replicas)]
        )
    for m, scalars in enumerate(all_scalars):
        step = 128
        for at in range(0, hidden_width, step):
            start = m * hidden_width + at
            total = scalars[0] * arrived_ref[0, start : start + step, :].astype(F32)
            for d in range(1, replicas):
                total = total + scalars[d] * arrived_ref[d, start : start + step, :].astype(F32)
            if m == 2:
                down_ref[at : at + step, :] = total
            else:
                (gate_ref, up_ref)[m][:, at : at + step] = total.T


def call(kernel, name, out_shapes, mib, scratch=(), specs=None, out_specs=None):
    more = {}
    if specs is not None:
        more["in_specs"] = specs
    if out_specs is not None:
        more["out_specs"] = out_specs
    return pl.pallas_call(
        kernel,
        name=name,
        out_shape=out_shapes,
        scratch_shapes=scratch,
        compiler_params=params(mib),
        **more,
    )


def per_device(tokens, routing, probs, cotangent, w_gate, w_up, w_down):
    experts = lax.axis_size("expert")
    replicas = lax.axis_size("dp")
    rows_here, top_count = routing.shape
    width = tokens.shape[1]
    hidden_width = w_gate.shape[2]
    capacity = 5 * rows_here * top_count // (4 * experts)
    slots = experts * capacity
    shard = width // replicas
    sent_rows = width // rows_here * 2 * capacity + 8
    shape = jax.ShapeDtypeStruct
    routing_rows = routing.T
    prob_rows = probs.T
    gate, up, down = w_gate[0], w_up[0], w_down[0]
    pinned = functools.partial(pltpu.with_memory_space_constraint, memory_space=pltpu.HBM)
    in_hbm = pl.BlockSpec(memory_space=pltpu.HBM)
    dma = pltpu.SemaphoreType.DMA

    send = call(
        functools.partial(dispatch_kernel, capacity),
        "dispatch", shape((experts, sent_rows, rows_here), BF16), 16,
        (
            pltpu.VMEM((top_count, rows_here), jnp.int32),
            pltpu.VMEM((top_count, rows_here), BF16),
            pltpu.VMEM((2 * rows_here, width), BF16),
            dma((2,)),
            dma((width // 256,)),
        ),
        specs=[in_hbm] * 4,
    )(pinned(routing_rows), pinned(prob_rows), pinned(tokens), pinned(cotangent))
    mixed = lax.all_to_all(send, "expert", 0, 0, tiled=True)
    blocks, back = call(
        functools.partial(expert_kernel, capacity),
        "expert",
        (
            pltpu.HBM((replicas, 3 * hidden_width, shard), BF16),
            pltpu.HBM((experts, rows_here + 8, width), BF16),
        ),
        44,
        (
            pltpu.VMEM((slots, width), BF16),
            pltpu.VMEM((slots, width), BF16),
            pltpu.VMEM((slots, width), BF16),
            pltpu.VMEM((experts, rows_here + 8, width), BF16),
            pltpu.VMEM((replicas, 3 * hidden_width, shard), BF16),
            dma((width // BACK_STEP,)),
            dma((2 * width // (4 * shard),)),
        ),
        specs=[VMEM] * 4,
        out_specs=(in_hbm, in_hbm),
    )(mixed, gate, up, down)
    back = lax.psum_scatter(
        back.reshape(experts * (rows_here + 8), width), "expert", scatter_dimension=0, tiled=True
    )
    arrived = lax.all_to_all(blocks, "dp", 0, 0, tiled=True)
    partial = call(
        functools.partial(gram_kernel, replicas),
        "gram", shape((replicas, replicas, 128), F32), 12,
    )(arrived)
    partials = lax.all_to_all(partial, "dp", 0, 0, tiled=True)
    grad_gate, grad_up, grad_down = call(
        functools.partial(combine_kernel, replicas),
        "combine",
        (
            shape((shard, hidden_width), F32),
            shape((shard, hidden_width), F32),
            shape((hidden_width, shard), F32),
        ),
        12,
    )(partials, arrived)
    grad_gate, back = lax.optimization_barrier((grad_gate, back))
    input_grad, router_grad = call(
        finish_kernel,
        "finish",
        (pltpu.HBM((rows_here, width), BF16), shape((top_count, rows_here), BF16)),
        4,
        (pltpu.VMEM((rows_here + 8, width), BF16), dma((5,)), dma((4,))),
        specs=[in_hbm, VMEM],
        out_specs=(in_hbm, VMEM),
    )(pinned(back), prob_rows)
    return (grad_gate[None], grad_up[None], grad_down[None], input_grad, router_grad.T)


def solution(mesh):
    placed = (
        P(("dp", "expert"), None),
        P(("dp", "expert"), None),
        P(("dp", "expert"), None),
        P(("dp", "expert"), None),
        P("expert", None, None),
        P("expert", None, None),
        P("expert", None, None),
    )
    return jax.shard_map(
        per_device,
        mesh=mesh,
        in_specs=placed,
        out_specs=(
            P("expert", "dp", None),
            P("expert", "dp", None),
            P("expert", None, "dp"),
            P(("dp", "expert"), None),
            P(("dp", "expert"), None),
        ),
        check_vma=False,
    )
```
